768 devices in a mesh: group: 48 (over x, z), peer: 16 (over y, core).
Axes of the slice: x: 4, y: 8, z: 12, core: 2. Of those that a mesh axis runs over, the one named last changes fastest.
Arguments:
- points: bfloat16 [786432, 256], P(('group', 'peer')), may hold values from -6 to 6
- cotangent: bfloat16 [786432, 256], P(('group', 'peer')), may hold values from -6 to 6
- dest_code: int32 [6144], P(('group', 'peer')), may hold values from 0 to 15, as said below
- src_code: int32 [6144], P(('group', 'peer')), may hold values from 0 to 15, as said below
- w_qkv: bfloat16 [256, 768], replicated
- w_out: bfloat16 [256, 256], replicated, may hold values from -0.375 to 0.375
- norm_attn: float32 [256], replicated, may hold values from 0.25 to 1.75
- norm_mlp: float32 [256], replicated, may hold values from 0.25 to 1.75
- w_hidden: bfloat16 [256, 1024], replicated, may hold values from -0.375 to 0.375
- w_output: bfloat16 [1024, 256], replicated, may hold values from -0.1875 to 0.1875
Outputs:
- block_out: bfloat16 [786432, 256], P(('group', 'peer'))
- hidden_grad: float32 [256, 1024], P(None, 'peer')
- output_grad: float32 [1024, 256], P('peer')
The draws below stay inside these ranges and needn't reach their ends.
Inputs may be any that keep to these rules, and one draw needn't show every extreme that they name: Within a device the entries are distinct; every device of a group receives exactly 8 blocks, and the sender's dest_code and the receiver's src_code name each moved block consistently. `src_code`: within a device the entries are distinct and name the blocks that dest_code sends to it.
All inputs are finite; a program needn't handle non-finite values.
Results may differ from the reference program's by a relative error of at most 0.014.
The reference program's roundings to bfloat16 on the way count: a program that leaves them out, or rounds other values in their place, can miss the bound.
Values may be sent and summed in bfloat16 or wider, within the bound.
A program may use at most 32 MiB of HBM per device.

```python
import jax
import jax.numpy as jnp
from jax import lax

D = 256
FF = 1024
HEAD_DIM = 16
BLOCK = 128
BLOCKS_DEV = 8
PATCH_BLOCKS = 4
HEADS = 16
CAP = 1
ROWS_DEV = 1024
POINTS = 786432
NBLK = 6144
N_GROUP = 48
N_PEER = 16


def redeal_tables(key):
    groups = NBLK // (N_PEER * BLOCKS_DEV)

    def one_group(group_key):
        first, second, third = jax.random.split(group_key, 3)
        codes = jax.random.permutation(first, N_PEER * CAP)[:BLOCKS_DEV].astype(jnp.int32)
        sender_order = jax.vmap(lambda k: jax.random.permutation(k, BLOCKS_DEV))(jax.random.split(second, N_PEER))
        slot_order = jax.vmap(lambda k: jax.random.permutation(k, BLOCKS_DEV))(jax.random.split(third, N_PEER))
        own = jnp.arange(N_PEER, dtype=jnp.int32)[:, None]
        sent = codes[sender_order]
        dest = (own + sent % N_PEER) % N_PEER * CAP + sent // N_PEER
        taken = codes[slot_order]
        src = (own - taken % N_PEER) % N_PEER * CAP + taken // N_PEER
        return (dest.astype(jnp.int32), src.astype(jnp.int32))
    dest, src = jax.vmap(one_group)(jax.random.split(jax.random.fold_in(key, 7), groups))
    return (dest.reshape(-1), src.reshape(-1))


def draw_dest_code(key, part):
    return redeal_tables(key)[0]


def draw_src_code(key, part):
    return redeal_tables(key)[1]


def draw_w_qkv(key, part):
    values = jax.random.normal(jax.random.fold_in(key, 11), (D, 3 * D), jnp.float32) * D ** (-0.5)
    return values.astype(jnp.bfloat16)


def block_scale(rng, extent, cuts, least, high):
    def one(dim, blocks):
        draws = jax.random.uniform(jax.random.fold_in(jax.random.fold_in(rng, 6), dim), (blocks,), jnp.float32, least / len(cuts), high / len(cuts))
        return jnp.repeat(jnp.exp(draws), extent[dim] // blocks).reshape((-1,) + (1,) * (len(extent) - dim - 1))

    level = one(*cuts[0])
    for cut in cuts[1:]:
        level = level * one(*cut)
    return level


def noise(rng, dims, scale, limit, cuts=(), held_as=jnp.bfloat16):
    array = jax.random.normal(rng, dims, jnp.float32) * scale
    if len(cuts) > 0:
        array = block_scale(rng, dims, cuts, -0.22, 0.18) * array
    return jnp.clip(array, min=-limit, max=limit).astype(held_as)


def setup_inputs(seed: int = 0) -> dict:
    key_list = jax.random.split(jax.random.key(seed), 11)
    points = noise(key_list[0], (POINTS, D), 1.0, 6.0, ((0, 768),))
    cotangent = noise(key_list[1], (POINTS, D), 1.0, 6.0, ((0, 768),))
    dest_code = draw_dest_code(jax.random.fold_in(key_list[10], 71), 0)
    src_code = draw_src_code(jax.random.fold_in(key_list[10], 71), 0)
    w_qkv = draw_w_qkv(jax.random.fold_in(key_list[10], 71), 0)
    w_out = noise(key_list[5], (D, D), D ** -0.5, 0.375)
    norm_attn = jnp.clip(1.0 + 0.15 * jax.random.normal(key_list[6], (D,), jnp.float32), 0.25, 1.75)
    norm_mlp = jnp.clip(1.0 + 0.15 * jax.random.normal(key_list[7], (D,), jnp.float32), 0.25, 1.75)
    w_hidden = noise(key_list[8], (D, FF), D ** -0.5, 0.375)
    w_output = noise(key_list[9], (FF, D), FF ** -0.5, 0.1875)
    return dict(points=points, cotangent=cotangent, dest_code=dest_code, src_code=src_code, w_qkv=w_qkv, w_out=w_out, norm_attn=norm_attn, norm_mlp=norm_mlp, w_hidden=w_hidden, w_output=w_output)


def layer_norm(v):
    centre = v - lax.optimization_barrier(jnp.mean(v, axis=-1, keepdims=True))
    spread = lax.optimization_barrier(jnp.mean(centre * centre, axis=-1, keepdims=True))
    return centre * lax.rsqrt(spread + 1e-05)

def source_blocks(dest_g, src_g):
    sender = src_g // CAP
    wanted = jnp.arange(N_PEER, dtype=jnp.int32)[:, None] * CAP + src_g % CAP
    rows = dest_g[sender]
    which = jnp.argmax((rows == wanted[..., None]).astype(jnp.int32), axis=-1).astype(jnp.int32)
    return (sender * BLOCKS_DEV + which).reshape(-1)

def device_layer(feats, cot, w_qkv, w_out, norm_attn, norm_mlp, w_hidden, w_output, grad_scale):
    rows = feats.shape[0]
    patch = PATCH_BLOCKS * BLOCK
    first = feats.astype(jnp.float32)
    normed = (layer_norm(first) * norm_attn).astype(jnp.bfloat16)
    qkv = jnp.dot(normed, w_qkv, preferred_element_type=jnp.float32).astype(jnp.bfloat16)
    shaped = qkv.astype(jnp.float32).reshape(rows // patch, patch, 3, HEADS, HEAD_DIM)
    query, keys, values = (shaped[:, :, 0], shaped[:, :, 1], shaped[:, :, 2])
    scores = jnp.einsum('pqhe,pkhe->phqk', query, keys) / jnp.sqrt(jnp.float32(HEAD_DIM))
    probs = jax.nn.softmax(scores, axis=-1).astype(jnp.bfloat16)
    att = jnp.einsum('phqk,pkhe->pqhe', probs.astype(jnp.float32), values).astype(jnp.bfloat16).reshape(rows, D)
    hidden_state = (first + jnp.dot(att, w_out, preferred_element_type=jnp.float32)).astype(jnp.bfloat16)
    second = (layer_norm(hidden_state.astype(jnp.float32)) * norm_mlp).astype(jnp.bfloat16)
    pre = jnp.dot(second, w_hidden, preferred_element_type=jnp.float32)
    act, gelu_back = jax.vjp(lambda v: jax.nn.gelu(v, approximate=True), pre)
    act = act.astype(jnp.bfloat16)
    result = (hidden_state.astype(jnp.float32) + jnp.dot(act, w_output, preferred_element_type=jnp.float32)).astype(jnp.bfloat16)
    out_term = jnp.einsum('rf,rd->fd', act.astype(jnp.float32), cot.astype(jnp.float32)) * grad_scale
    dact = jnp.dot(cot, w_output.T, preferred_element_type=jnp.float32)
    dpre = gelu_back(dact)[0].astype(jnp.bfloat16)
    hid_term = jnp.einsum('rd,rf->df', second.astype(jnp.float32), dpre.astype(jnp.float32)) * grad_scale
    return (result, hid_term, out_term)

def reference(points, cotangent, dest_code, src_code, w_qkv, w_out, norm_attn, norm_mlp, w_hidden, w_output):
    groups = N_GROUP
    dest = dest_code.reshape(groups, N_PEER, BLOCKS_DEV)
    src = src_code.reshape(groups, N_PEER, BLOCKS_DEV)
    flat = jax.vmap(source_blocks)(dest, src)
    blocks = points.reshape(groups, N_PEER * BLOCKS_DEV, BLOCK, D)
    cot_blocks = cotangent.reshape(groups, N_PEER * BLOCKS_DEV, BLOCK, D)
    hil = jax.vmap(lambda b, f: b[f])(blocks, flat).reshape(groups * N_PEER, ROWS_DEV, D)
    hil_cot = jax.vmap(lambda b, f: b[f])(cot_blocks, flat).reshape(groups * N_PEER, ROWS_DEV, D)
    grad_scale = 1.0 / jnp.sqrt(jnp.float32(POINTS))

    def step(carry, item):
        res, hid_term, out_term = device_layer(item[0], item[1], w_qkv, w_out, norm_attn, norm_mlp, w_hidden, w_output, grad_scale)
        return ((carry[0] + hid_term, carry[1] + out_term), res)
    init = (jnp.zeros((D, FF), jnp.float32), jnp.zeros((FF, D), jnp.float32))
    (hidden_grad, output_grad), outs = lax.scan(step, init, (hil, hil_cot))
    outs = outs.reshape(groups, N_PEER * BLOCKS_DEV, BLOCK, D)
    back = jax.vmap(lambda o, f: jnp.zeros_like(o).at[f].set(o))(outs, flat)
    return (back.reshape(POINTS, D), hidden_grad, output_grad)
```

```python
import jax
import jax.numpy as jnp
from jax import lax
from jax.sharding import PartitionSpec as P

D = 256
HEAD_DIM = 16
PATCH_BLOCKS = 4


def layer_norm(v):
    centre = v - jnp.mean(v, axis=-1, keepdims=True)
    spread = jnp.mean(centre * centre, axis=-1, keepdims=True)
    return centre * lax.rsqrt(spread + 1e-05)


def pack_blocks(arr, codes, slots, block_rows):
    width = arr.shape[1]
    pieces = arr.reshape(codes.shape[0], block_rows, width)
    return jnp.zeros((slots, block_rows, width), arr.dtype).at[codes].set(pieces)


def split_heads(mat, patches, patch, heads):
    return (
        mat.reshape(patches, patch, heads, HEAD_DIM)
        .transpose(0, 2, 1, 3)
        .reshape(patches * heads, patch, HEAD_DIM)
    )


def patch_attention(qkv, rows, patch):
    heads = D // HEAD_DIM
    patches = rows // patch
    query = split_heads(qkv[:, :D], patches, patch, heads)
    keys = split_heads(qkv[:, D : 2 * D], patches, patch, heads)
    values = split_heads(qkv[:, 2 * D :], patches, patch, heads)
    factor = 1.0 / jnp.sqrt(jnp.float32(HEAD_DIM))

    def one_head(triple):
        scores = (
            jnp.einsum("qe,ke->qk", triple[0], triple[1], preferred_element_type=jnp.float32)
            * factor
        )
        probs = jax.nn.softmax(scores, axis=-1).astype(jnp.bfloat16)
        return jnp.einsum("qk,ke->qe", probs, triple[2], preferred_element_type=jnp.float32).astype(
            jnp.bfloat16
        )

    mixed = lax.map(one_head, (query, keys, values), batch_size=4)
    return mixed.reshape(patches, heads, patch, HEAD_DIM).transpose(0, 2, 1, 3).reshape(rows, D)


def attend(feats, w_qkv, norm_attn, rows, patch):
    normed = (layer_norm(feats.astype(jnp.float32)) * norm_attn).astype(jnp.bfloat16)
    qkv = jnp.dot(normed, w_qkv, preferred_element_type=jnp.float32).astype(jnp.bfloat16)
    return patch_attention(qkv, rows, patch)


def mlp_terms(hidden_state, cot, norm_mlp, w_hidden, w_output):
    second = (layer_norm(hidden_state.astype(jnp.float32)) * norm_mlp).astype(jnp.bfloat16)
    pre = jnp.dot(second, w_hidden, preferred_element_type=jnp.float32)
    act, gelu_back = jax.vjp(lambda v: jax.nn.gelu(v, approximate=True), pre)
    act = act.astype(jnp.bfloat16)
    result = (
        hidden_state.astype(jnp.float32)
        + jnp.dot(act, w_output, preferred_element_type=jnp.float32)
    ).astype(jnp.bfloat16)
    out_term = jnp.einsum("rf,rd->fd", act, cot, preferred_element_type=jnp.float32)
    dact = jnp.einsum("rd,fd->rf", cot, w_output, preferred_element_type=jnp.float32)
    dpre = gelu_back(dact)[0].astype(jnp.bfloat16)
    hid_term = jnp.einsum("rf,rd->fd", dpre, second, preferred_element_type=jnp.float32)
    return (result, hid_term, out_term)


def redeal(blocks, send_codes, take_codes, slots, block_rows):
    buf = pack_blocks(blocks, send_codes, slots, block_rows)
    got = lax.all_to_all(buf, "peer", split_axis=0, concat_axis=0, tiled=True)
    return jnp.take(got, take_codes, axis=0).reshape(blocks.shape)


def swap(pieces, axis):
    return lax.all_to_all(pieces, axis, split_axis=0, concat_axis=0, tiled=True)


def sum_grads(hid_term, out_term, peers, groups, scale):
    units = hid_term.shape[0] // peers
    both = jnp.concatenate(
        [hid_term.reshape(peers, units, D), out_term.reshape(peers, units, D)], axis=1
    ).astype(jnp.bfloat16)
    share = jnp.sum(swap(both, "peer").astype(jnp.float32), axis=0) * scale
    flat = share.reshape(-1, 8, 128)
    pieces = flat.shape[0]
    per = -(-pieces // groups)
    padded = jnp.pad(flat, ((0, per * groups - pieces), (0, 0), (0, 0)))
    mine = jnp.sum(
        swap(padded, "group").reshape(groups, per, 8, 128), axis=0
    )
    everyone = jnp.broadcast_to(mine[None], (groups, per, 8, 128)).reshape(groups * per, 8, 128)
    total = swap(everyone, "group")[:pieces].reshape(2 * units, D)
    return total[:units].T, total[units:]


def per_device(
    points, cotangent, dest_code, src_code, w_qkv, w_out, norm_attn, norm_mlp, w_hidden, w_output
):
    peers = lax.axis_size("peer")
    groups = lax.axis_size("group")
    blocks_here = dest_code.shape[0]
    rows = points.shape[0]
    block_rows = rows // blocks_here
    slots = peers * ((blocks_here + peers - 1) // peers)
    patch = PATCH_BLOCKS * block_rows
    grad_scale = 1.0 / jnp.sqrt(jnp.float32(rows * peers * groups))
    feats = redeal(points, dest_code, src_code, slots, block_rows)
    att = attend(feats, w_qkv, norm_attn, rows, patch)
    att = redeal(att, src_code, dest_code, slots, block_rows)
    hidden_state = (
        points.astype(jnp.float32) + jnp.dot(att, w_out, preferred_element_type=jnp.float32)
    ).astype(jnp.bfloat16)
    result, hid_term, out_term = mlp_terms(hidden_state, cotangent, norm_mlp, w_hidden, w_output)
    hidden_grad, output_grad = sum_grads(hid_term, out_term, peers, groups, grad_scale)
    return (result, hidden_grad, output_grad)


def solution(mesh):
    return jax.shard_map(
        per_device,
        mesh=mesh,
        in_specs=(
            P(("group", "peer"), None),
            P(("group", "peer"), None),
            P(("group", "peer")),
            P(("group", "peer")),
            P(),
            P(),
            P(),
            P(),
            P(),
            P(),
        ),
        out_specs=(P(("group", "peer"), None), P(None, "peer"), P("peer", None)),
        check_vma=False,
    )
```

```python
import functools

import jax
import jax.numpy as jnp
import numpy as np
from jax import lax
from jax.experimental import pallas as pl
from jax.experimental.pallas import tpu as pltpu
from jax.sharding import PartitionSpec as P

MESH = pl.DeviceIdType.MESH

D = 256
HEAD_DIM = 16
PATCH_BLOCKS = 4


def layer_norm(v):
    centre = v - jnp.mean(v, axis=-1, keepdims=True)
    spread = jnp.mean(centre * centre, axis=-1, keepdims=True)
    return centre * lax.rsqrt(spread + 1e-05)


def pack_blocks(arr, codes, slots, block_rows):
    width = arr.shape[1]
    pieces = arr.reshape(codes.shape[0], block_rows, width)
    return jnp.zeros((slots, block_rows, width), arr.dtype).at[codes].set(pieces)


def split_heads(mat, patches, patch, heads):
    return (
        mat.reshape(patches, patch, heads, HEAD_DIM)
        .transpose(0, 2, 1, 3)
        .reshape(patches * heads, patch, HEAD_DIM)
    )


def patch_attention(qkv, rows, patch):
    heads = D // HEAD_DIM
    patches = rows // patch
    query = split_heads(qkv[:, :D], patches, patch, heads)
    keys = split_heads(qkv[:, D : 2 * D], patches, patch, heads)
    values = split_heads(qkv[:, 2 * D :], patches, patch, heads)
    factor = 1.0 / jnp.sqrt(jnp.float32(HEAD_DIM))

    def one_head(triple):
        scores = (
            jnp.einsum("qe,ke->qk", triple[0], triple[1], preferred_element_type=jnp.float32)
            * factor
        )
        probs = jax.nn.softmax(scores, axis=-1).astype(jnp.bfloat16)
        return jnp.einsum("qk,ke->qe", probs, triple[2], preferred_element_type=jnp.float32).astype(
            jnp.bfloat16
        )

    mixed = lax.map(one_head, (query, keys, values), batch_size=4)
    return mixed.reshape(patches, heads, patch, HEAD_DIM).transpose(0, 2, 1, 3).reshape(rows, D)


def attend(feats, w_qkv, norm_attn, rows, patch):
    normed = (layer_norm(feats.astype(jnp.float32)) * norm_attn).astype(jnp.bfloat16)
    qkv = jnp.dot(normed, w_qkv, preferred_element_type=jnp.float32).astype(jnp.bfloat16)
    return patch_attention(qkv, rows, patch)


def mlp_terms(hidden_state, cot, norm_mlp, w_hidden, w_output):
    second = (layer_norm(hidden_state.astype(jnp.float32)) * norm_mlp).astype(jnp.bfloat16)
    pre = jnp.dot(second, w_hidden, preferred_element_type=jnp.float32)
    act, gelu_back = jax.vjp(lambda v: jax.nn.gelu(v, approximate=True), pre)
    act = act.astype(jnp.bfloat16)
    result = (
        hidden_state.astype(jnp.float32)
        + jnp.dot(act, w_output, preferred_element_type=jnp.float32)
    ).astype(jnp.bfloat16)
    out_term = jnp.einsum("rf,rd->fd", act, cot, preferred_element_type=jnp.float32)
    dact = jnp.einsum("rd,fd->rf", cot, w_output, preferred_element_type=jnp.float32)
    dpre = gelu_back(dact)[0].astype(jnp.bfloat16)
    hid_term = jnp.einsum("rf,rd->fd", dpre, second, preferred_element_type=jnp.float32)
    return (result, hid_term, out_term)


def redeal(blocks, send_codes, take_codes, slots, block_rows):
    buf = pack_blocks(blocks, send_codes, slots, block_rows)
    got = lax.all_to_all(buf, "peer", split_axis=0, concat_axis=0, tiled=True)
    return jnp.take(got, take_codes, axis=0).reshape(blocks.shape)


def gradient_kernel(peers, xs, zs, scale, terms, out, pair_in, y_out, y_in, x_out, x_in, z_all, x_all,
                    pair_send, pair_recv, y_send, y_recv, x_send, x_recv, z_send, z_recv, g_send, g_recv):
    ys = peers // 2
    peer, group = lax.axis_index("peer"), lax.axis_index("group")
    y, core = peer // 2, peer % 2
    x, z = group // zs, group % zs
    rows = terms.shape[1]
    part = rows // xs

    def on_core(other):
        return {"peer": y * 2 + other, "group": group}

    def on_y(other):
        return {"peer": other * 2 + core, "group": group}

    def on_x(other):
        return {"peer": peer, "group": other * zs + z}

    def on_z(other):
        return {"peer": peer, "group": x * zs + other}

    def send(src, dst, send_sem, recv_sem, device):
        copy = pltpu.make_async_remote_copy(
            src_ref=src, dst_ref=dst, send_sem=send_sem, recv_sem=recv_sem,
            device_id=device, device_id_type=MESH,
        )
        copy.start()
        return copy

    partners = [on_core(1 - core)]
    partners += [on_y((y + k) % ys) for k in range(1, ys)]
    partners += [on_x((x + k) % xs) for k in range(1, xs)]
    partners += [on_z((z + k) % zs) for k in range(1, zs)]
    barrier = pltpu.get_barrier_semaphore()
    for device in partners:
        pl.semaphore_signal(barrier, inc=1, device_id=device, device_id_type=MESH)
    pl.semaphore_wait(barrier, len(partners))

    order = list(range(1, ys)) + [0]
    pair = {}
    for k in order:
        owner = (y + k) % ys
        pair[k] = send(terms.at[owner * 2 + (1 - core)], pair_in.at[k], pair_send.at[k], pair_recv.at[k],
                       on_core(1 - core))
    along_y = {}
    for k in order:
        owner = (y + k) % ys
        pair[k].wait_recv()
        both = terms[owner * 2 + core].astype(jnp.float32) + pair_in[k].astype(jnp.float32)
        if k:
            y_out[k - 1] = both.astype(jnp.bfloat16)
            along_y[k] = send(y_out.at[k - 1], y_in.at[k - 1], y_send.at[k - 1], y_recv.at[k - 1], on_y(owner))
    total = both
    for k in range(1, ys):
        along_y[k].wait_recv()
        total = total + y_in[k - 1].astype(jnp.float32)
    x_out[...] = total.astype(jnp.bfloat16).reshape(xs, part, D)
    along_x = [
        send(x_out.at[(x + k) % xs], x_in.at[k - 1], x_send.at[k - 1], x_recv.at[k - 1], on_x((x + k) % xs))
        for k in range(1, xs)
    ]
    mine = x_out[x].astype(jnp.float32)
    for k in range(1, xs):
        along_x[k - 1].wait_recv()
        mine = mine + x_in[k - 1].astype(jnp.float32)
    z_all[z] = mine.astype(jnp.bfloat16)
    along_z = [
        send(z_all.at[z], z_all.at[z], z_send.at[k - 1], z_recv.at[k - 1], on_z((z + k) % zs))
        for k in range(1, zs)
    ]
    for copy in along_z:
        copy.wait_recv()
    whole = z_all[0].astype(jnp.float32)
    for k in range(1, zs):
        whole = whole + z_all[k].astype(jnp.float32)
    x_all[x] = whole * scale
    back = [
        send(x_all.at[x], x_all.at[x], g_send.at[k - 1], g_recv.at[k - 1], on_x((x + k) % xs))
        for k in range(1, xs)
    ]
    for copy in back:
        copy.wait_recv()
    out[...] = x_all[...].reshape(rows, D)
    for copy in [*pair.values(), *along_y.values(), *along_x, *along_z, *back]:
        copy.wait_send()


def sum_grads(terms, peers, groups, scale):
    xs = 4 if groups % 4 == 0 else 1
    ys, zs = peers // 2, groups // xs
    rows = terms.shape[1]
    dma = pltpu.SemaphoreType.DMA
    bf16 = jnp.bfloat16
    return pl.pallas_call(
        functools.partial(gradient_kernel, peers, xs, zs, scale),
        out_shape=jax.ShapeDtypeStruct((rows, D), jnp.float32),
        in_specs=[pl.BlockSpec(memory_space=pltpu.VMEM)],
        out_specs=pl.BlockSpec(memory_space=pltpu.VMEM),
        scratch_shapes=[
            pltpu.VMEM((ys, rows, D), bf16),
            pltpu.VMEM((ys - 1, rows, D), bf16),
            pltpu.VMEM((ys - 1, rows, D), bf16),
            pltpu.VMEM((xs, rows // xs, D), bf16),
            pltpu.VMEM((max(xs - 1, 1), rows // xs, D), bf16),
            pltpu.VMEM((zs, rows // xs, D), bf16),
            pltpu.VMEM((xs, rows // xs, D), jnp.float32),
            dma((ys,)), dma((ys,)),
            dma((ys - 1,)), dma((ys - 1,)),
            dma((max(xs - 1, 1),)), dma((max(xs - 1, 1),)),
            dma((max(zs - 1, 1),)), dma((max(zs - 1, 1),)),
            dma((max(xs - 1, 1),)), dma((max(xs - 1, 1),)),
        ],
        compiler_params=pltpu.CompilerParams(
            collective_id=0, has_side_effects=True, vmem_limit_bytes=32 << 20
        ),
        cost_estimate=pl.CostEstimate(flops=1 << 24, bytes_accessed=64 << 20, transcendentals=0),
    )(terms)


def per_device(
    points, cotangent, dest_code, src_code, w_qkv, w_out, norm_attn, norm_mlp, w_hidden, w_output
):
    peers = lax.axis_size("peer")
    groups = lax.axis_size("group")
    blocks_here = dest_code.shape[0]
    rows = points.shape[0]
    block_rows = rows // blocks_here
    slots = peers * ((blocks_here + peers - 1) // peers)
    patch = PATCH_BLOCKS * block_rows
    grad_scale = float(1.0 / np.sqrt(np.float32(rows * peers * groups)))
    feats = redeal(points, dest_code, src_code, slots, block_rows)
    att = attend(feats, w_qkv, norm_attn, rows, patch)
    att = redeal(att, src_code, dest_code, slots, block_rows)
    hidden_state = (
        points.astype(jnp.float32) + jnp.dot(att, w_out, preferred_element_type=jnp.float32)
    ).astype(jnp.bfloat16)
    result, hid_term, out_term = mlp_terms(hidden_state, cotangent, norm_mlp, w_hidden, w_output)
    units = hid_term.shape[0] // peers
    terms = jnp.concatenate(
        [hid_term.reshape(peers, units, D), out_term.reshape(peers, units, D)], axis=1
    ).astype(jnp.bfloat16)
    sums = sum_grads(terms, peers, groups, grad_scale)
    hidden_grad, output_grad = sums[:units].T, sums[units:]
    return (result, hidden_grad, output_grad)


def solution(mesh):
    return jax.shard_map(
        per_device,
        mesh=mesh,
        in_specs=(
            P(("group", "peer"), None),
            P(("group", "peer"), None),
            P(("group", "peer")),
            P(("group", "peer")),
            P(),
            P(),
            P(),
            P(),
            P(),
            P(),
        ),
        out_specs=(P(("group", "peer"), None), P(None, "peer"), P("peer", None)),
        check_vma=False,
    )
```

```python
import functools

import jax
import jax.numpy as jnp
import numpy as np
from jax import lax
from jax.experimental import pallas as pl
from jax.experimental.pallas import tpu as pltpu
from jax.sharding import PartitionSpec as P

MESH = pl.DeviceIdType.MESH

D = 256
HEAD_DIM = 16
PATCH_BLOCKS = 4
LANES = 128


def layer_norm(v):
    centre = v - jnp.mean(v, axis=-1, keepdims=True)
    spread = jnp.mean(centre * centre, axis=-1, keepdims=True)
    return centre * lax.rsqrt(spread + 1e-05)


def start_send(src, dst, send_sem, recv_sem, device):
    copy = pltpu.make_async_remote_copy(
        src_ref=src, dst_ref=dst, send_sem=send_sem, recv_sem=recv_sem,
        device_id=device, device_id_type=MESH,
    )
    copy.start()
    return copy


def block_for(codes, peer):
    which = jnp.int32(0)
    for i in range(codes.shape[0]):
        which = jnp.where(codes[i] == peer, i, which)
    return which


def heads_of_lanes(qkv, att, first_row, rows, lanes):
    head_of_lane = lax.broadcasted_iota(jnp.int32, (1, LANES), 1) // HEAD_DIM
    ones = jnp.ones((rows, LANES), jnp.bfloat16)
    factor = 1.4426950408889634 / HEAD_DIM**0.5
    tile = rows // 2
    zero = jnp.bfloat16(0)

    def one_head(head, carry):
        mine = head_of_lane == head
        keys = qkv[first_row : first_row + rows, D + lanes : D + lanes + LANES]
        values = qkv[first_row : first_row + rows, 2 * D + lanes : 2 * D + lanes + LANES]
        values = jnp.concatenate([jnp.where(mine, values, zero), ones], axis=1)
        for start in range(first_row, first_row + rows, tile):
            query = jnp.where(mine, qkv[start : start + tile, lanes : lanes + LANES], zero)
            scores = lax.dot_general(
                query, keys, (((1,), (1,)), ((), ())), preferred_element_type=jnp.float32
            )
            top = jnp.max(scores, axis=1, keepdims=True)
            weights = jnp.exp2((scores - top) * factor).astype(jnp.bfloat16)
            mixed = jnp.dot(weights, values, preferred_element_type=jnp.float32)
            att[start : start + tile] += mixed[:, :LANES] / mixed[:, LANES:]
        return carry

    lax.fori_loop(0, LANES // HEAD_DIM, one_head, 0, unroll=LANES // HEAD_DIM)


def attention_kernel(peers, points, dest, src, w_qkv, w_out, norm_attn, out, normed, stage, got, feats,
                     qkv, att, mixed, back_stage, back, whole, send_sem, recv_sem, back_send, back_recv):
    group, me = lax.axis_index("group"), lax.axis_index("peer")
    blocks, block_rows = points.shape[0], points.shape[1]
    patch = PATCH_BLOCKS * block_rows
    others = [(me + k) % peers for k in range(1, peers)]

    def at(peer):
        return {"group": group, "peer": peer}

    barrier = pltpu.get_barrier_semaphore()
    for peer in others:
        pl.semaphore_signal(barrier, inc=1, device_id=at(peer), device_id_type=MESH)
    for i in range(blocks):
        normed[i] = (layer_norm(points[i].astype(jnp.float32)) * norm_attn[...]).astype(jnp.bfloat16)
    for k, peer in enumerate(others):
        stage[k] = normed[block_for(dest, peer)]
    got[me] = normed[block_for(dest, me)]
    pl.semaphore_wait(barrier, peers - 1)
    sent = [
        start_send(stage.at[k], got.at[me], send_sem.at[k], recv_sem.at[k], at(peer))
        for k, peer in enumerate(others)
    ]
    for copy in sent:
        copy.wait_recv()
    for j in range(blocks):
        feats[j * block_rows : (j + 1) * block_rows] = got[src[j]]
    qkv[...] = jnp.dot(feats[...], w_qkv[...], preferred_element_type=jnp.float32).astype(jnp.bfloat16)
    for part in range(D // LANES):
        att[...] = jnp.zeros_like(att)
        for first_row in range(0, blocks * block_rows, patch):
            heads_of_lanes(qkv, att, first_row, patch, part * LANES)
        mixed[part] = att[...].astype(jnp.bfloat16).reshape(blocks, block_rows, LANES)
        for k, peer in enumerate(others):
            back_stage[part, k] = mixed[part, block_for(src, peer)]
            sent.append(
                start_send(back_stage.at[part, k], back.at[part, me], back_send.at[part, k],
                           back_recv.at[part, k], at(peer))
            )
        back[part, me] = mixed[part, block_for(src, me)]
    for copy in sent[peers - 1 :]:
        copy.wait_recv()
    for part in range(D // LANES):
        for i in range(blocks):
            whole[i * block_rows : (i + 1) * block_rows, part * LANES : (part + 1) * LANES] = back[part, dest[i]]
    added = jnp.dot(whole[...], w_out[...], preferred_element_type=jnp.float32)
    for i in range(blocks):
        out[i] = (points[i].astype(jnp.float32) + added[i * block_rows : (i + 1) * block_rows]).astype(jnp.bfloat16)
    for copy in sent:
        copy.wait_send()


def attend(points, dest_code, src_code, w_qkv, w_out, norm_attn, peers):
    blocks = dest_code.shape[0]
    rows = points.shape[0]
    block_rows = rows // blocks
    parts = D // LANES
    vmem, smem = pl.BlockSpec(memory_space=pltpu.VMEM), pl.BlockSpec(memory_space=pltpu.SMEM)
    dma, bf16 = pltpu.SemaphoreType.DMA, jnp.bfloat16
    return pl.pallas_call(
        functools.partial(attention_kernel, peers),
        out_shape=jax.ShapeDtypeStruct((blocks, block_rows, D), bf16),
        in_specs=[vmem, smem, smem, vmem, vmem, vmem],
        out_specs=vmem,
        scratch_shapes=[
            pltpu.VMEM((blocks, block_rows, D), bf16),
            pltpu.VMEM((peers - 1, block_rows, D), bf16),
            pltpu.VMEM((peers, block_rows, D), bf16),
            pltpu.VMEM((rows, D), bf16),
            pltpu.VMEM((rows, 3 * D), bf16),
            pltpu.VMEM((rows, LANES), jnp.float32),
            pltpu.VMEM((parts, blocks, block_rows, LANES), bf16),
            pltpu.VMEM((parts, peers - 1, block_rows, LANES), bf16),
            pltpu.VMEM((parts, peers, block_rows, LANES), bf16),
            pltpu.VMEM((rows, D), bf16),
            dma((peers - 1,)), dma((peers - 1,)),
            dma((parts, peers - 1)), dma((parts, peers - 1)),
        ],
        compiler_params=pltpu.CompilerParams(
            collective_id=1, has_side_effects=True, vmem_limit_bytes=48 << 20
        ),
        cost_estimate=pl.CostEstimate(flops=1 << 32, bytes_accessed=4 << 20, transcendentals=1 << 23),
    )(points.reshape(blocks, block_rows, D), dest_code, src_code, w_qkv, w_out, norm_attn.reshape(1, D)).reshape(rows, D)


def mlp_terms(hidden_state, cot, norm_mlp, w_hidden, w_output):
    second = (layer_norm(hidden_state.astype(jnp.float32)) * norm_mlp).astype(jnp.bfloat16)
    pre = jnp.dot(second, w_hidden, preferred_element_type=jnp.float32)
    act, gelu_back = jax.vjp(lambda v: jax.nn.gelu(v, approximate=True), pre)
    act = act.astype(jnp.bfloat16)
    result = (
        hidden_state.astype(jnp.float32)
        + jnp.dot(act, w_output, preferred_element_type=jnp.float32)
    ).astype(jnp.bfloat16)
    out_term = jnp.einsum("rf,rd->fd", act, cot, preferred_element_type=jnp.float32)
    dact = jnp.einsum("rd,fd->rf", cot, w_output, preferred_element_type=jnp.float32)
    dpre = gelu_back(dact)[0].astype(jnp.bfloat16)
    hid_term = jnp.einsum("rf,rd->fd", dpre, second, preferred_element_type=jnp.float32)
    return (result, hid_term, out_term)


def gradient_kernel(peers, xs, zs, scale, terms, out, pair_in, y_out, y_in, x_out, x_in, z_all, x_all,
                    pair_send, pair_recv, y_send, y_recv, x_send, x_recv, z_send, z_recv, g_send, g_recv):
    ys = peers // 2
    peer, group = lax.axis_index("peer"), lax.axis_index("group")
    y, core = peer // 2, peer % 2
    x, z = group // zs, group % zs
    rows = terms.shape[1]
    part = rows // xs

    def on_core(other):
        return {"peer": y * 2 + other, "group": group}

    def on_y(other):
        return {"peer": other * 2 + core, "group": group}

    def on_x(other):
        return {"peer": peer, "group": other * zs + z}

    def on_z(other):
        return {"peer": peer, "group": x * zs + other}

    def send(src, dst, send_sem, recv_sem, device):
        copy = pltpu.make_async_remote_copy(
            src_ref=src, dst_ref=dst, send_sem=send_sem, recv_sem=recv_sem,
            device_id=device, device_id_type=MESH,
        )
        copy.start()
        return copy

    partners = [on_core(1 - core)]
    partners += [on_y((y + k) % ys) for k in range(1, ys)]
    partners += [on_x((x + k) % xs) for k in range(1, xs)]
    partners += [on_z((z + k) % zs) for k in range(1, zs)]
    barrier = pltpu.get_barrier_semaphore()
    for device in partners:
        pl.semaphore_signal(barrier, inc=1, device_id=device, device_id_type=MESH)
    pl.semaphore_wait(barrier, len(partners))

    order = list(range(1, ys)) + [0]
    pair = {}
    for k in order:
        owner = (y + k) % ys
        pair[k] = send(terms.at[owner * 2 + (1 - core)], pair_in.at[k], pair_send.at[k], pair_recv.at[k],
                       on_core(1 - core))
    along_y = {}
    for k in order:
        owner = (y + k) % ys
        pair[k].wait_recv()
        both = terms[owner * 2 + core].astype(jnp.float32) + pair_in[k].astype(jnp.float32)
        if k:
            y_out[k - 1] = both.astype(jnp.bfloat16)
            along_y[k] = send(y_out.at[k - 1], y_in.at[k - 1], y_send.at[k - 1], y_recv.at[k - 1], on_y(owner))
    total = both
    for k in range(1, ys):
        along_y[k].wait_recv()
        total = total + y_in[k - 1].astype(jnp.float32)
    x_out[...] = total.astype(jnp.bfloat16).reshape(xs, part, D)
    along_x = [
        send(x_out.at[(x + k) % xs], x_in.at[k - 1], x_send.at[k - 1], x_recv.at[k - 1], on_x((x + k) % xs))
        for k in range(1, xs)
    ]
    mine = x_out[x].astype(jnp.float32)
    for k in range(1, xs):
        along_x[k - 1].wait_recv()
        mine = mine + x_in[k - 1].astype(jnp.float32)
    z_all[z] = mine.astype(jnp.bfloat16)
    along_z = [
        send(z_all.at[z], z_all.at[z], z_send.at[k - 1], z_recv.at[k - 1], on_z((z + k) % zs))
        for k in range(1, zs)
    ]
    for copy in along_z:
        copy.wait_recv()
    whole = z_all[0].astype(jnp.float32)
    for k in range(1, zs):
        whole = whole + z_all[k].astype(jnp.float32)
    x_all[x] = whole * scale
    back = [
        send(x_all.at[x], x_all.at[x], g_send.at[k - 1], g_recv.at[k - 1], on_x((x + k) % xs))
        for k in range(1, xs)
    ]
    for copy in back:
        copy.wait_recv()
    out[...] = x_all[...].reshape(rows, D)
    for copy in [*pair.values(), *along_y.values(), *along_x, *along_z, *back]:
        copy.wait_send()


def sum_grads(terms, peers, groups, scale):
    xs = 4 if groups % 4 == 0 else 1
    ys, zs = peers // 2, groups // xs
    rows = terms.shape[1]
    dma = pltpu.SemaphoreType.DMA
    bf16 = jnp.bfloat16
    return pl.pallas_call(
        functools.partial(gradient_kernel, peers, xs, zs, scale),
        out_shape=jax.ShapeDtypeStruct((rows, D), jnp.float32),
        in_specs=[pl.BlockSpec(memory_space=pltpu.VMEM)],
        out_specs=pl.BlockSpec(memory_space=pltpu.VMEM),
        scratch_shapes=[
            pltpu.VMEM((ys, rows, D), bf16),
            pltpu.VMEM((ys - 1, rows, D), bf16),
            pltpu.VMEM((ys - 1, rows, D), bf16),
            pltpu.VMEM((xs, rows // xs, D), bf16),
            pltpu.VMEM((max(xs - 1, 1), rows // xs, D), bf16),
            pltpu.VMEM((zs, rows // xs, D), bf16),
            pltpu.VMEM((xs, rows // xs, D), jnp.float32),
            dma((ys,)), dma((ys,)),
            dma((ys - 1,)), dma((ys - 1,)),
            dma((max(xs - 1, 1),)), dma((max(xs - 1, 1),)),
            dma((max(zs - 1, 1),)), dma((max(zs - 1, 1),)),
            dma((max(xs - 1, 1),)), dma((max(xs - 1, 1),)),
        ],
        compiler_params=pltpu.CompilerParams(
            collective_id=0, has_side_effects=True, vmem_limit_bytes=32 << 20
        ),
        cost_estimate=pl.CostEstimate(flops=1 << 24, bytes_accessed=64 << 20, transcendentals=0),
    )(terms)


def per_device(
    points, cotangent, dest_code, src_code, w_qkv, w_out, norm_attn, norm_mlp, w_hidden, w_output
):
    peers = lax.axis_size("peer")
    groups = lax.axis_size("group")
    rows = points.shape[0]
    grad_scale = float(1.0 / np.sqrt(np.float32(rows * peers * groups)))
    hidden_state = attend(points, dest_code, src_code, w_qkv, w_out, norm_attn, peers)
    result, hid_term, out_term = mlp_terms(hidden_state, cotangent, norm_mlp, w_hidden, w_output)
    units = hid_term.shape[0] // peers
    terms = jnp.concatenate(
        [hid_term.reshape(peers, units, D), out_term.reshape(peers, units, D)], axis=1
    ).astype(jnp.bfloat16)
    sums = sum_grads(terms, peers, groups, grad_scale)
    hidden_grad, output_grad = sums[:units].T, sums[units:]
    return (result, hidden_grad, output_grad)


def solution(mesh):
    return jax.shard_map(
        per_device,
        mesh=mesh,
        in_specs=(
            P(("group", "peer"), None),
            P(("group", "peer"), None),
            P(("group", "peer")),
            P(("group", "peer")),
            P(),
            P(),
            P(),
            P(),
            P(),
            P(),
        ),
        out_specs=(P(("group", "peer"), None), P(None, "peer"), P("peer", None)),
        check_vma=False,
    )
```

```python
import functools

import jax
import jax.numpy as jnp
import numpy as np
from jax import lax
from jax.experimental import pallas as pl
from jax.experimental.pallas import tpu as pltpu
from jax.sharding import PartitionSpec as P

D = 256
HEAD_DIM = 16
PATCH_BLOCKS = 4
LANES = 128
HALF = 64
UNITS = 256
MESH = pl.DeviceIdType.MESH
F32, BF16 = jnp.float32, jnp.bfloat16


def layer_norm(v):
    centre = v - jnp.mean(v, axis=-1, keepdims=True)
    spread = jnp.mean(centre * centre, axis=-1, keepdims=True)
    return centre * lax.rsqrt(spread + 1e-05)


def dot(a, b):
    return jnp.dot(a, b, preferred_element_type=F32)


def dot_rows(a, b):
    return lax.dot_general(a, b, (((1,), (1,)), ((), ())), preferred_element_type=F32)


def gelu_and_slope(x):
    root = 0.7978845608028654
    square = x * x
    bend = jnp.tanh(x * (root + (root * 0.044715) * square))
    half = 0.5 + 0.5 * bend
    slope = half + (0.5 * x) * (1.0 - bend * bend) * (root + (3 * root * 0.044715) * square)
    return x * half, slope


def start_send(src, dst, send_sem, recv_sem, device):
    copy = pltpu.make_async_remote_copy(
        src_ref=src, dst_ref=dst, send_sem=send_sem, recv_sem=recv_sem,
        device_id=device, device_id_type=MESH,
    )
    copy.start()
    return copy


def block_for(codes, peer):
    which = jnp.int32(0)
    for i in range(codes.shape[0]):
        which = jnp.where(codes[i] == peer, i, which)
    return which


def some_heads(qkv, att, first_row, rows, lanes, heads):
    head_of_lane = lax.broadcasted_iota(jnp.int32, (1, LANES), 1) // HEAD_DIM
    ones = jnp.ones((rows, LANES), BF16)
    factor = 1.4426950408889634 / HEAD_DIM**0.5
    tile = rows // 2
    zero = jnp.bfloat16(0)

    def one_head(head, carry):
        mine = head_of_lane == head
        keys = qkv[first_row : first_row + rows, D + lanes : D + lanes + LANES]
        values = qkv[first_row : first_row + rows, 2 * D + lanes : 2 * D + lanes + LANES]
        values = jnp.concatenate([jnp.where(mine, values, zero), ones], axis=1)
        for start in range(first_row, first_row + rows, tile):
            query = jnp.where(mine, qkv[start : start + tile, lanes : lanes + LANES], zero)
            scores = dot_rows(query, keys)
            top = jnp.max(scores, axis=1, keepdims=True)
            weights = jnp.exp2((scores - top) * factor).astype(BF16)
            mixed = dot(weights, values)
            att[start : start + tile] += mixed[:, :LANES] / mixed[:, LANES:]
        return carry

    lax.fori_loop(heads[0], heads[1], one_head, 0, unroll=heads[1] - heads[0])


def swap_halves(upper, lower, first):
    low = lax.broadcasted_iota(jnp.int32, (1, LANES), 1) < HALF
    if first:
        return jnp.where(low, upper, pltpu.roll(lower, HALF, 1))
    return jnp.where(low, pltpu.roll(upper, HALF, 1), lower)


def block_kernel(peers, xs, zs, scale, points_any, cot_any, dest, src, w_qkv_any, w_out_any, norm_attn,
                 norm_mlp, w_hidden_any, w_output_any, out_any, hidden_grad, output_grad,
                 points, cot, w_qkv, w_out, w_hidden, w_output, w_hidden_t, w_output_t,
                 normed, stage, got, feats, qkv, att, packed, back_stage, back, whole, hidden, second,
                 dact, result, answer, terms, pair_in, x_out, x_in, y_out, y_in, z_all, x_all,
                 load_sem, send_sem, recv_sem, back_send, back_recv, pair_send, pair_recv,
                 x_send, x_recv, y_send, y_recv, z_send, z_recv, g_send, g_recv, out_sem):
    loads = [
        pltpu.make_async_copy(a, b, load_sem.at[i])
        for i, (a, b) in enumerate(
            [(points_any, points), (w_qkv_any, w_qkv), (w_out_any, w_out), (cot_any, cot),
             (w_hidden_any, w_hidden), (w_output_any, w_output)]
        )
    ]
    for load in loads:
        load.start()
    group, me = lax.axis_index("group"), lax.axis_index("peer")
    ys = peers // 2
    y, core = me // 2, me % 2
    x, z = group // zs, group % zs
    blocks, block_rows = points.shape[0], points.shape[1]
    rows = blocks * block_rows
    patch = PATCH_BLOCKS * block_rows
    others = [(me + k) % peers for k in range(1, peers)]

    def at(peer):
        return {"group": group, "peer": peer}

    def on_x(other):
        return {"group": other * zs + z, "peer": me}

    def on_z(other):
        return {"group": x * zs + other, "peer": me}

    partners = [at(peer) for peer in others]
    partners += [on_x((x + k) % xs) for k in range(1, xs)]
    partners += [on_z((z + k) % zs) for k in range(1, zs)]
    barrier = pltpu.get_barrier_semaphore()
    for device in partners:
        pl.semaphore_signal(barrier, inc=1, device_id=device, device_id_type=MESH)

    loads[0].wait()
    for i in range(blocks):
        normed[i] = (layer_norm(points[i].astype(F32)) * norm_attn[...]).astype(BF16)
    for k, peer in enumerate(others):
        stage[k] = normed[block_for(dest, peer)]
    got[me] = normed[block_for(dest, me)]
    pl.semaphore_wait(barrier, len(partners))
    sent = [
        start_send(stage.at[k], got.at[me], send_sem.at[k], recv_sem.at[k], at(peer))
        for k, peer in enumerate(others)
    ]
    for load in loads[1:]:
        load.wait()
    w_hidden_t[...] = w_hidden[...].astype(F32).T.astype(BF16)
    w_output_t[...] = w_output[...].astype(F32).T.astype(BF16)
    dact[...] = dot_rows(w_output[...], cot[...])
    for copy in sent:
        copy.wait_recv()

    for j in range(blocks):
        feats[j * block_rows : (j + 1) * block_rows] = got[src[j]]
    qkv[...] = dot(feats[...], w_qkv[...]).astype(BF16)
    returned = []
    per_part = LANES // HEAD_DIM // 2
    for part in range(D // HALF):
        group_lanes, first = part // 2 * LANES, part % 2 == 0
        head = part % 2 * per_part
        att[...] = jnp.zeros_like(att)
        for first_row in range(0, rows, patch):
            some_heads(qkv, att, first_row, patch, group_lanes, (head, head + per_part))
        for j in range(blocks):
            start = j * block_rows
            packed[part, j] = swap_halves(
                att[start : start + HALF], att[start + HALF : start + block_rows], first
            ).astype(BF16)
        for k, peer in enumerate(others):
            back_stage[part, k] = packed[part, block_for(src, peer)]
            returned.append(
                start_send(back_stage.at[part, k], back.at[part, me], back_send.at[part, k],
                           back_recv.at[part, k], at(peer))
            )
        back[part, me] = packed[part, block_for(src, me)]
    for copy in returned:
        copy.wait_recv()
    for i in range(blocks):
        start = i * block_rows
        for lanes in range(D // LANES):
            even = back[2 * lanes, dest[i]].astype(F32)
            odd = back[2 * lanes + 1, dest[i]].astype(F32)
            cols = slice(lanes * LANES, (lanes + 1) * LANES)
            whole[start : start + HALF, cols] = swap_halves(even, odd, True).astype(BF16)
            whole[start + HALF : start + block_rows, cols] = swap_halves(even, odd, False).astype(BF16)
    for i in range(blocks):
        span = slice(i * block_rows, (i + 1) * block_rows)
        h = (points[i].astype(F32) + dot(whole[span], w_out[...])).astype(BF16)
        hidden[span] = h
        second[span] = (layer_norm(h.astype(F32)) * norm_mlp[...]).astype(BF16)

    chunks = w_hidden_t.shape[0] // UNITS
    share = UNITS * peers // w_hidden_t.shape[0]
    units = UNITS // share
    pairs = share // 2
    quarter = 2 * units // xs
    pair, along_x = [], []

    def to_pair(chunk):
        for j in range(pairs):
            pair.append(
                start_send(terms.at[chunk * share + 2 * j + (1 - core)], pair_in.at[chunk * pairs + j],
                           pair_send.at[chunk * pairs + j], pair_recv.at[chunk * pairs + j], at(y * 2 + 1 - core))
            )

    def to_x(chunk):
        for j in range(pairs):
            pair[chunk * pairs + j].wait_recv()
            both = terms[chunk * share + 2 * j + core].astype(F32) + pair_in[chunk * pairs + j].astype(F32)
            both = both.astype(BF16)
            for t in range(xs):
                x_out[chunk, t, j] = both[t * quarter : (t + 1) * quarter]
        for k in range(1, xs):
            along_x.append(
                start_send(x_out.at[chunk, (x + k) % xs], x_in.at[chunk, k - 1], x_send.at[chunk, k - 1],
                           x_recv.at[chunk, k - 1], on_x((x + k) % xs))
            )

    tile = UNITS
    for chunk in range(chunks):
        span = slice(chunk * UNITS, (chunk + 1) * UNITS)
        out_sum = hid_sum = None
        for start in range(0, rows, tile):
            these = slice(start, start + tile)
            act, slope = gelu_and_slope(dot_rows(w_hidden_t[span], second[these]))
            act = act.astype(BF16)
            dpre = (dact[span, these] * slope).astype(BF16)
            added = dot(w_output_t[:, span], act)
            result[:, these] = added if chunk == 0 else result[:, these] + added
            out_part, hid_part = dot(act, cot[these]), dot(dpre, second[these])
            out_sum = out_part if out_sum is None else out_sum + out_part
            hid_sum = hid_part if hid_sum is None else hid_sum + hid_part
        for j in range(share):
            mine = slice(j * units, (j + 1) * units)
            terms[chunk * share + j, :units] = hid_sum[mine].astype(BF16)
            terms[chunk * share + j, units:] = out_sum[mine].astype(BF16)
        to_pair(chunk)
        if chunk:
            to_x(chunk - 1)
    to_x(chunks - 1)
    for start in range(0, rows, tile):
        these = slice(start, start + tile)
        answer[these] = (hidden[these].astype(F32) + result[:, these].T).astype(BF16)
    store = pltpu.make_async_copy(answer, out_any, out_sem)
    store.start()

    for copy in along_x:
        copy.wait_recv()
    for chunk in range(chunks):
        for j in range(pairs):
            mine = x_out[chunk, x, j].astype(F32)
            for k in range(xs - 1):
                mine = mine + x_in[chunk, k, j].astype(F32)
            y_out[chunk * pairs + j] = mine.astype(BF16)
    along_y = [
        start_send(y_out.at[(y + k) % ys], y_in.at[k - 1], y_send.at[k - 1], y_recv.at[k - 1],
                   at((y + k) % ys * 2 + core))
        for k in range(1, ys)
    ]
    mine = y_out[y].astype(F32)
    for k, copy in enumerate(along_y):
        copy.wait_recv()
        mine = mine + y_in[k].astype(F32)
    z_all[z] = mine.astype(BF16)
    along_z = [
        start_send(z_all.at[z], z_all.at[z], z_send.at[k - 1], z_recv.at[k - 1], on_z((z + k) % zs))
        for k in range(1, zs)
    ]
    for copy in along_z:
        copy.wait_recv()
    total = z_all[0].astype(F32)
    for k in range(1, zs):
        total = total + z_all[k].astype(F32)
    x_all[x] = total * scale
    last = [
        start_send(x_all.at[x], x_all.at[x], g_send.at[k - 1], g_recv.at[k - 1], on_x((x + k) % xs))
        for k in range(1, xs)
    ]
    for copy in last:
        copy.wait_recv()
    sums = x_all[...].reshape(2 * units, D)
    hidden_grad[...] = sums[:units].T
    output_grad[...] = sums[units:]
    for copy in [*sent, *returned, *pair, *along_x, *along_y, *along_z, *last]:
        copy.wait_send()
    store.wait()


def per_device(
    points, cotangent, dest_code, src_code, w_qkv, w_out, norm_attn, norm_mlp, w_hidden, w_output
):
    peers, groups = lax.axis_size("peer"), lax.axis_size("group")
    xs = 4 if groups % 4 == 0 else 1
    ys, zs = peers // 2, groups // xs
    blocks, rows = dest_code.shape[0], points.shape[0]
    block_rows, ff = rows // blocks, w_output.shape[0]
    scale = float(1.0 / np.sqrt(np.float32(rows * peers * groups)))
    units = ff // peers
    chunks, pairs = ff // UNITS, UNITS // units // 2
    quarter = 2 * units // xs
    parts = D // HALF
    vmem, smem = pl.BlockSpec(memory_space=pltpu.VMEM), pl.BlockSpec(memory_space=pltpu.SMEM)
    far = pl.BlockSpec(memory_space=pl.ANY)
    dma = pltpu.SemaphoreType.DMA
    some = max(xs - 1, 1)
    held = lambda shape, dtype=BF16: pltpu.VMEM(shape, dtype)
    result, hidden_grad, output_grad = pl.pallas_call(
        functools.partial(block_kernel, peers, xs, zs, scale),
        out_shape=(
            jax.ShapeDtypeStruct((rows, D), BF16),
            jax.ShapeDtypeStruct((D, units), F32),
            jax.ShapeDtypeStruct((units, D), F32),
        ),
        in_specs=[far, far, smem, smem, far, far, vmem, vmem, far, far],
        out_specs=(far, vmem, vmem),
        scratch_shapes=[
            held((blocks, block_rows, D)), held((rows, D)), held((D, 3 * D)), held((D, D)),
            held((D, ff)), held((ff, D)), held((ff, D)), held((D, ff)),
            held((blocks, block_rows, D)), held((peers - 1, block_rows, D)), held((peers, block_rows, D)),
            held((rows, D)), held((rows, 3 * D)), held((rows, LANES), F32),
            held((parts, blocks, block_rows // 2, LANES)),
            held((parts, peers - 1, block_rows // 2, LANES)),
            held((parts, peers, block_rows // 2, LANES)),
            held((rows, D)), held((rows, D)), held((rows, D)),
            held((ff, rows), F32), held((D, rows), F32), held((rows, D)),
            held((peers, 2 * units, D)), held((ys, 2 * units, D)),
            held((chunks, xs, pairs, quarter, D)), held((chunks, some, pairs, quarter, D)),
            held((ys, quarter, D)), held((ys - 1, quarter, D)),
            held((zs, quarter, D)), held((xs, quarter, D), F32),
            dma((6,)), dma((peers - 1,)), dma((peers - 1,)),
            dma((parts, peers - 1)), dma((parts, peers - 1)),
            dma((ys,)), dma((ys,)), dma((chunks, some)), dma((chunks, some)),
            dma((ys - 1,)), dma((ys - 1,)), dma((max(zs - 1, 1),)), dma((max(zs - 1, 1),)),
            dma((some,)), dma((some,)), dma(()),
        ],
        compiler_params=pltpu.CompilerParams(
            collective_id=0, has_side_effects=True, vmem_limit_bytes=56 << 20
        ),
        cost_estimate=pl.CostEstimate(flops=1 << 33, bytes_accessed=4 << 20, transcendentals=1 << 23),
    )(points.reshape(blocks, block_rows, D), cotangent, dest_code, src_code, w_qkv, w_out,
      norm_attn.reshape(1, D), norm_mlp.reshape(1, D), w_hidden, w_output)
    return result, hidden_grad, output_grad


def solution(mesh):
    return jax.shard_map(
        per_device,
        mesh=mesh,
        in_specs=(
            P(("group", "peer"), None),
            P(("group", "peer"), None),
            P(("group", "peer")),
            P(("group", "peer")),
            P(),
            P(),
            P(),
            P(),
            P(),
            P(),
        ),
        out_specs=(P(("group", "peer"), None), P(None, "peer"), P("peer", None)),
        check_vma=False,
    )
```

```python
import functools

import jax
import jax.numpy as jnp
import numpy as np
from jax import lax
from jax.experimental import pallas as pl
from jax.experimental.pallas import tpu as pltpu
from jax.sharding import PartitionSpec as P

D = 256
HEAD_DIM = 16
PATCH_BLOCKS = 4
LANES = 128
PARTS = 4
SENDS = 2
UNITS = 256
MESH = pl.DeviceIdType.MESH
F32, BF16 = jnp.float32, jnp.bfloat16


def layer_norm(v):
    centre = v - jnp.mean(v, axis=-1, keepdims=True)
    spread = jnp.mean(centre * centre, axis=-1, keepdims=True)
    return centre * lax.rsqrt(spread + 1e-05)


def dot(a, b):
    return jnp.dot(a, b, preferred_element_type=F32)


def dot_rows(a, b):
    return lax.dot_general(a, b, (((1,), (1,)), ((), ())), preferred_element_type=F32)


def gelu_and_slope(x):
    root = 0.7978845608028654
    square = x * x
    bend = jnp.tanh(x * (root + (root * 0.044715) * square))
    half = 0.5 + 0.5 * bend
    slope = half + (0.5 * x) * (1.0 - bend * bend) * (root + (3 * root * 0.044715) * square)
    return x * half, slope


def start_send(src, dst, send_sem, recv_sem, device):
    copy = pltpu.make_async_remote_copy(
        src_ref=src, dst_ref=dst, send_sem=send_sem, recv_sem=recv_sem,
        device_id=device, device_id_type=MESH,
    )
    copy.start()
    return copy


def block_for(codes, peer):
    which = jnp.int32(0)
    for i in range(codes.shape[0]):
        which = jnp.where(codes[i] == peer, i, which)
    return which


def some_queries(qkv, att, first_key, keys_count, first_query, queries, first_out):
    head_of_lane = lax.broadcasted_iota(jnp.int32, (1, LANES), 1) // HEAD_DIM
    ones = jnp.ones((keys_count, LANES), BF16)
    factor = 1.4426950408889634 / HEAD_DIM**0.5
    zero = jnp.bfloat16(0)
    patch = slice(first_key, first_key + keys_count)
    these = slice(first_query, first_query + queries)
    outs = slice(first_out, first_out + queries)
    for lanes in range(0, D, LANES):

        def one_head(head, carry):
            mine = head_of_lane == head
            keys = qkv[patch, D + lanes : D + lanes + LANES]
            values = qkv[patch, 2 * D + lanes : 2 * D + lanes + LANES]
            values = jnp.concatenate([jnp.where(mine, values, zero), ones], axis=1)
            query = jnp.where(mine, qkv[these, lanes : lanes + LANES], zero)
            scores = dot_rows(query, keys)
            top = jnp.max(scores, axis=1, keepdims=True)
            weights = jnp.exp2((scores - top) * factor).astype(BF16)
            mixed = dot(weights, values)
            att[outs, lanes : lanes + LANES] += mixed[:, :LANES] / mixed[:, LANES:]
            return carry

        lax.fori_loop(0, LANES // HEAD_DIM, one_head, 0, unroll=LANES // HEAD_DIM)


def block_kernel(peers, xs, zs, scale, points_any, cot_any, dest, src, w_qkv_any, w_out_any, norm_attn,
                 norm_mlp, w_hidden_any, w_output_any, out_any, hidden_grad, output_grad,
                 points, cot, w_qkv, w_out, w_hidden, w_output, w_hidden_t, w_output_t,
                 cot_parts, normed, stage, got, feats, qkv, att, packed, back_stage, back, second,
                 dact, result, answer, out_acc, hid_acc, terms, pair_in, x_out, x_in, y_out, y_in, z_all, x_all,
                 load_sem, send_sem, recv_sem, back_send, back_recv, pair_send, pair_recv,
                 x_send, x_recv, y_send, y_recv, z_send, z_recv, g_send, g_recv, out_sem):
    loads = [
        pltpu.make_async_copy(a, b, load_sem.at[i])
        for i, (a, b) in enumerate(
            [(points_any, points), (w_qkv_any, w_qkv), (w_out_any, w_out), (cot_any, cot),
             (w_hidden_any, w_hidden), (w_output_any, w_output)]
        )
    ]
    for load in loads:
        load.start()
    group, me = lax.axis_index("group"), lax.axis_index("peer")
    ys = peers // 2
    y, core = me // 2, me % 2
    x, z = group // zs, group % zs
    blocks, block_rows = points.shape[0], points.shape[1]
    rows = blocks * block_rows
    patch = PATCH_BLOCKS * block_rows
    others = [(me + k) % peers for k in range(1, peers)]

    def at(peer):
        return {"group": group, "peer": peer}

    def on_x(other):
        return {"group": other * zs + z, "peer": me}

    def on_z(other):
        return {"group": x * zs + other, "peer": me}

    partners = [at(peer) for peer in others]
    partners += [on_x((x + k) % xs) for k in range(1, xs)]
    partners += [on_z((z + k) % zs) for k in range(1, zs)]
    barrier = pltpu.get_barrier_semaphore()
    for device in partners:
        pl.semaphore_signal(barrier, inc=1, device_id=device, device_id_type=MESH)

    loads[0].wait()
    step = block_rows // SENDS
    sent = []
    for part in range(SENDS):
        span = slice(part * step, (part + 1) * step)
        for i in range(blocks):
            normed[part, i] = (layer_norm(points[i, span].astype(F32)) * norm_attn[...]).astype(BF16)
        for k, peer in enumerate(others):
            stage[part, k] = normed[part, block_for(dest, peer)]
        got[part][me] = normed[part, block_for(dest, me)]
        if part == 0:
            pl.semaphore_wait(barrier, len(partners))
        for k, peer in enumerate(others):
            sent.append(
                start_send(stage.at[part, k], got[part].at[me], send_sem.at[part, k], recv_sem.at[part, k],
                           at(peer))
            )
    for load in loads[1:]:
        load.wait()
    piece = block_rows // PARTS
    part_rows = blocks * piece
    for part in range(PARTS):
        for i in range(blocks):
            cot_parts[part, i * piece : (i + 1) * piece] = cot[
                i * block_rows + part * piece : i * block_rows + (part + 1) * piece
            ]
    w_hidden_t[...] = w_hidden[...].astype(F32).T.astype(BF16)
    w_output_t[...] = w_output[...].astype(F32).T.astype(BF16)
    for part in range(PARTS):
        dact[:, part * part_rows : (part + 1) * part_rows] = dot_rows(w_output[...], cot_parts[part])

    query_rows = PATCH_BLOCKS * piece
    pieces_sent = PARTS // SENDS
    for part in range(SENDS):
        for copy in sent[part * (peers - 1) : (part + 1) * (peers - 1)]:
            copy.wait_recv()
        for j in range(blocks):
            block = got[part][src[j]]
            for q in range(pieces_sent):
                start = j // PATCH_BLOCKS * patch + (part * pieces_sent + q) * query_rows + j % PATCH_BLOCKS * piece
                feats[start : start + piece] = block[q * piece : (q + 1) * piece]
        for first in range(0, rows, patch):
            these = slice(first + part * patch // SENDS, first + (part + 1) * patch // SENDS)
            qkv[these] = dot(feats[these], w_qkv[...]).astype(BF16)

    returned = []
    for part in range(PARTS):
        att[...] = jnp.zeros_like(att)
        for n in range(rows // patch):
            some_queries(qkv, att, n * patch, patch, n * patch + part * query_rows, query_rows, n * query_rows)
        packed[part] = att[...].astype(BF16).reshape(blocks, piece, D)
        for k, peer in enumerate(others):
            back_stage[part, k] = packed[part, block_for(src, peer)]
            returned.append(
                start_send(back_stage.at[part, k], back[part].at[me], back_send.at[part, k],
                           back_recv.at[part, k], at(peer))
            )
        back[part][me] = packed[part, block_for(src, me)]

    chunks = w_hidden_t.shape[0] // UNITS
    share = UNITS * peers // w_hidden_t.shape[0]
    units = UNITS // share
    pairs = share // 2
    quarter = 2 * units // xs
    pair, along_x = [], []

    def to_pair(chunk):
        for j in range(pairs):
            pair.append(
                start_send(terms.at[chunk * share + 2 * j + (1 - core)], pair_in.at[chunk * pairs + j],
                           pair_send.at[chunk * pairs + j], pair_recv.at[chunk * pairs + j], at(y * 2 + 1 - core))
            )

    def to_x(chunk):
        for j in range(pairs):
            pair[chunk * pairs + j].wait_recv()
            both = terms[chunk * share + 2 * j + core].astype(F32) + pair_in[chunk * pairs + j].astype(F32)
            both = both.astype(BF16)
            for t in range(xs):
                x_out[chunk, t, j] = both[t * quarter : (t + 1) * quarter]
        for k in range(1, xs):
            along_x.append(
                start_send(x_out.at[chunk, (x + k) % xs], x_in.at[chunk, k - 1], x_send.at[chunk, k - 1],
                           x_recv.at[chunk, k - 1], on_x((x + k) % xs))
            )

    for part in range(PARTS):
        for copy in returned[part * (peers - 1) : (part + 1) * (peers - 1)]:
            copy.wait_recv()
        mixed = jnp.concatenate([back[part][dest[i]] for i in range(blocks)], axis=0)
        before = jnp.concatenate([points[i, part * piece : (part + 1) * piece] for i in range(blocks)], axis=0)
        hidden = (before.astype(F32) + dot(mixed, w_out[...])).astype(BF16)
        second[...] = (layer_norm(hidden.astype(F32)) * norm_mlp[...]).astype(BF16)
        these = slice(part * part_rows, (part + 1) * part_rows)
        for chunk in range(chunks):
            span = slice(chunk * UNITS, (chunk + 1) * UNITS)
            act, slope = gelu_and_slope(dot_rows(w_hidden_t[span], second[...]))
            act = act.astype(BF16)
            dpre = (dact[span, these] * slope).astype(BF16)
            out_part, hid_part = dot(act, cot_parts[part]), dot(dpre, second[...])
            if part:
                out_part, hid_part = out_acc[span] + out_part, hid_acc[span] + hid_part
            if part < PARTS - 1:
                out_acc[span], hid_acc[span] = out_part, hid_part
            else:
                for j in range(share):
                    mine = slice(j * units, (j + 1) * units)
                    terms[chunk * share + j, :units] = hid_part[mine].astype(BF16)
                    terms[chunk * share + j, units:] = out_part[mine].astype(BF16)
                to_pair(chunk)
                if chunk:
                    to_x(chunk - 1)
            added = dot(w_output_t[:, span], act)
            result[...] = added if chunk == 0 else result[...] + added
        if part == PARTS - 1:
            to_x(chunks - 1)
        ended = (hidden.astype(F32) + result[...].T).astype(BF16)
        for i in range(blocks):
            answer[i, part * piece : (part + 1) * piece] = ended[i * piece : (i + 1) * piece]
    store = pltpu.make_async_copy(answer, out_any, out_sem)
    store.start()

    for copy in along_x:
        copy.wait_recv()
    for chunk in range(chunks):
        for j in range(pairs):
            mine = x_out[chunk, x, j].astype(F32)
            for k in range(xs - 1):
                mine = mine + x_in[chunk, k, j].astype(F32)
            y_out[chunk * pairs + j] = mine.astype(BF16)
    along_y = [
        start_send(y_out.at[(y + k) % ys], y_in.at[k - 1], y_send.at[k - 1], y_recv.at[k - 1],
                   at((y + k) % ys * 2 + core))
        for k in range(1, ys)
    ]
    mine = y_out[y].astype(F32)
    for k, copy in enumerate(along_y):
        copy.wait_recv()
        mine = mine + y_in[k].astype(F32)
    z_all[z] = mine.astype(BF16)
    along_z = [
        start_send(z_all.at[z], z_all.at[z], z_send.at[k - 1], z_recv.at[k - 1], on_z((z + k) % zs))
        for k in range(1, zs)
    ]
    for copy in along_z:
        copy.wait_recv()
    total = z_all[0].astype(F32)
    for k in range(1, zs):
        total = total + z_all[k].astype(F32)
    x_all[x] = total * scale
    last = [
        start_send(x_all.at[x], x_all.at[x], g_send.at[k - 1], g_recv.at[k - 1], on_x((x + k) % xs))
        for k in range(1, xs)
    ]
    for copy in last:
        copy.wait_recv()
    sums = x_all[...].reshape(2 * units, D)
    hidden_grad[...] = sums[:units]
    output_grad[...] = sums[units:]
    for copy in [*sent, *returned, *pair, *along_x, *along_y, *along_z, *last]:
        copy.wait_send()
    store.wait()


def per_device(
    points, cotangent, dest_code, src_code, w_qkv, w_out, norm_attn, norm_mlp, w_hidden, w_output
):
    peers, groups = lax.axis_size("peer"), lax.axis_size("group")
    xs = 4 if groups % 4 == 0 else 1
    ys, zs = peers // 2, groups // xs
    blocks, rows = dest_code.shape[0], points.shape[0]
    block_rows, ff = rows // blocks, w_output.shape[0]
    scale = float(1.0 / np.sqrt(np.float32(rows * peers * groups)))
    units = ff // peers
    chunks, pairs = ff // UNITS, UNITS // units // 2
    quarter = 2 * units // xs
    vmem, smem = pl.BlockSpec(memory_space=pltpu.VMEM), pl.BlockSpec(memory_space=pltpu.SMEM)
    far = pl.BlockSpec(memory_space=pl.ANY)
    dma = pltpu.SemaphoreType.DMA
    some = max(xs - 1, 1)
    held = lambda shape, dtype=BF16: pltpu.VMEM(shape, dtype)
    result, hidden_grad, output_grad = pl.pallas_call(
        functools.partial(block_kernel, peers, xs, zs, scale),
        out_shape=(
            jax.ShapeDtypeStruct((blocks, block_rows, D), BF16),
            jax.ShapeDtypeStruct((units, D), F32),
            jax.ShapeDtypeStruct((units, D), F32),
        ),
        in_specs=[far, far, smem, smem, far, far, vmem, vmem, far, far],
        out_specs=(far, vmem, vmem),
        scratch_shapes=[
            held((blocks, block_rows, D)), held((rows, D)), held((D, 3 * D)), held((D, D)),
            held((D, ff)), held((ff, D)), held((ff, D)), held((D, ff)),
            held((PARTS, rows // PARTS, D)),
            held((SENDS, blocks, block_rows // SENDS, D)),
            held((SENDS, peers - 1, block_rows // SENDS, D)),
            (held((peers, block_rows // SENDS, D)),) * SENDS,
            held((rows, D)), held((rows, 3 * D)), held((rows // PARTS, D), F32),
            held((PARTS, blocks, block_rows // PARTS, D)),
            held((PARTS, peers - 1, block_rows // PARTS, D)),
            (held((peers, block_rows // PARTS, D)),) * PARTS,
            held((rows // PARTS, D)),
            held((ff, rows), F32), held((D, rows // PARTS), F32), held((blocks, block_rows, D)),
            held((ff, D), F32), held((ff, D), F32),
            held((peers, 2 * units, D)), held((ys, 2 * units, D)),
            held((chunks, xs, pairs, quarter, D)), held((chunks, some, pairs, quarter, D)),
            held((ys, quarter, D)), held((ys - 1, quarter, D)),
            held((zs, quarter, D)), held((xs, quarter, D), F32),
            dma((6,)), dma((SENDS, peers - 1)), dma((SENDS, peers - 1)),
            dma((PARTS, peers - 1)), dma((PARTS, peers - 1)),
            dma((ys,)), dma((ys,)), dma((chunks, some)), dma((chunks, some)),
            dma((ys - 1,)), dma((ys - 1,)), dma((max(zs - 1, 1),)), dma((max(zs - 1, 1),)),
            dma((some,)), dma((some,)), dma(()),
        ],
        compiler_params=pltpu.CompilerParams(
            collective_id=0, has_side_effects=True, vmem_limit_bytes=56 << 20
        ),
        cost_estimate=pl.CostEstimate(flops=1 << 33, bytes_accessed=4 << 20, transcendentals=1 << 23),
    )(points.reshape(blocks, block_rows, D), cotangent, dest_code, src_code, w_qkv, w_out,
      norm_attn.reshape(1, D), norm_mlp.reshape(1, D), w_hidden, w_output)
    return result.reshape(rows, D), hidden_grad.T, output_grad


def solution(mesh):
    return jax.shard_map(
        per_device,
        mesh=mesh,
        in_specs=(
            P(("group", "peer"), None),
            P(("group", "peer"), None),
            P(("group", "peer")),
            P(("group", "peer")),
            P(),
            P(),
            P(),
            P(),
            P(),
            P(),
        ),
        out_specs=(P(("group", "peer"), None), P(None, "peer"), P("peer", None)),
        check_vma=False,
    )
```

```python
import functools

import jax
import jax.numpy as jnp
import numpy as np
from jax import lax
from jax.experimental import pallas as pl
from jax.experimental.pallas import tpu as pltpu
from jax.sharding import PartitionSpec as P

D = 256
HEAD_DIM = 16
PATCH_BLOCKS = 4
LANES = 128
PARTS = 4
SENDS = 2
UNITS = 256
MESH = pl.DeviceIdType.MESH
F32, BF16 = jnp.float32, jnp.bfloat16


def layer_norm(v):
    centre = v - jnp.mean(v, axis=-1, keepdims=True)
    spread = jnp.mean(centre * centre, axis=-1, keepdims=True)
    return centre * lax.rsqrt(spread + 1e-05)


def dot(a, b):
    return jnp.dot(a, b, preferred_element_type=F32)


def dot_rows(a, b):
    return lax.dot_general(a, b, (((1,), (1,)), ((), ())), preferred_element_type=F32)


def gelu_and_slope(x):
    root = 0.7978845608028654
    square = x * x
    bend = jnp.tanh(x * (root + (root * 0.044715) * square))
    half = 0.5 + 0.5 * bend
    slope = half + (0.5 * x) * (1.0 - bend * bend) * (root + (3 * root * 0.044715) * square)
    return x * half, slope


def start_send(src, dst, send_sem, recv_sem, device):
    copy = pltpu.make_async_remote_copy(
        src_ref=src, dst_ref=dst, send_sem=send_sem, recv_sem=recv_sem,
        device_id=device, device_id_type=MESH,
    )
    copy.start()
    return copy


def block_for(codes, peer):
    which = jnp.int32(0)
    for i in range(codes.shape[0]):
        which = jnp.where(codes[i] == peer, i, which)
    return which


def some_queries(qkv, att, first_key, keys_count, first_query, queries, first_out):
    head_of_lane = lax.broadcasted_iota(jnp.int32, (1, LANES), 1) // HEAD_DIM
    ones = jnp.ones((keys_count, LANES), BF16)
    factor = 1.4426950408889634 / HEAD_DIM**0.5
    zero = jnp.bfloat16(0)
    patch = slice(first_key, first_key + keys_count)
    these = slice(first_query, first_query + queries)
    outs = slice(first_out, first_out + queries)
    for lanes in range(0, D, LANES):

        def one_head(head, carry):
            mine = head_of_lane == head
            keys = qkv[patch, D + lanes : D + lanes + LANES]
            values = qkv[patch, 2 * D + lanes : 2 * D + lanes + LANES]
            values = jnp.concatenate([jnp.where(mine, values, zero), ones], axis=1)
            query = jnp.where(mine, qkv[these, lanes : lanes + LANES], zero)
            scores = dot_rows(query, keys)
            top = jnp.max(scores, axis=1, keepdims=True)
            weights = jnp.exp2((scores - top) * factor).astype(BF16)
            mixed = dot(weights, values)
            att[outs, lanes : lanes + LANES] += mixed[:, :LANES] / mixed[:, LANES:]
            return carry

        lax.fori_loop(0, LANES // HEAD_DIM, one_head, 0, unroll=LANES // HEAD_DIM)


def block_kernel(peers, xs, zs, scale, points_any, cot_any, dest, src, w_qkv_any, w_out_any, norm_attn,
                 norm_mlp, w_hidden_any, w_output_any, out_any, hidden_grad, output_grad,
                 points, cot, w_qkv, w_out, w_hidden, w_output, w_hidden_t, w_output_t,
                 cot_parts, normed, stage, got, feats, qkv, att, packed, back_stage, back, second,
                 dact, result, answer, out_acc, hid_acc, terms, pair_in, x_out, x_in, y_out, y_in, z_all, x_all,
                 load_sem, send_sem, recv_sem, back_send, back_recv, pair_send, pair_recv,
                 x_send, x_recv, y_send, y_recv, z_send, z_recv, g_send, g_recv, out_sem):
    loads = [
        pltpu.make_async_copy(a, b, load_sem.at[i])
        for i, (a, b) in enumerate(
            [(points_any, points), (w_qkv_any, w_qkv), (w_out_any, w_out), (cot_any, cot),
             (w_hidden_any, w_hidden), (w_output_any, w_output)]
        )
    ]
    for load in loads:
        load.start()
    group, me = lax.axis_index("group"), lax.axis_index("peer")
    ys = peers // 2
    y, core = me // 2, me % 2
    x, z = group // zs, group % zs
    blocks, block_rows = points.shape[0], points.shape[1]
    rows = blocks * block_rows
    patch = PATCH_BLOCKS * block_rows
    others = [(me + k) % peers for k in range(1, peers)]

    def at(peer):
        return {"group": group, "peer": peer}

    def on_x(other):
        return {"group": other * zs + z, "peer": me}

    def on_z(other):
        return {"group": x * zs + other, "peer": me}

    partners = [at(peer) for peer in others]
    partners += [on_x((x + k) % xs) for k in range(1, xs)]
    partners += [on_z((z + k) % zs) for k in range(1, zs)]
    barrier = pltpu.get_barrier_semaphore()
    for device in partners:
        pl.semaphore_signal(barrier, inc=1, device_id=device, device_id_type=MESH)

    loads[0].wait()
    step = block_rows // SENDS
    sent = []
    for part in range(SENDS):
        span = slice(part * step, (part + 1) * step)
        for i in range(blocks):
            normed[part, i] = (layer_norm(points[i, span].astype(F32)) * norm_attn[...]).astype(BF16)
        for k, peer in enumerate(others):
            stage[part, k] = normed[part, block_for(dest, peer)]
        got[part][me] = normed[part, block_for(dest, me)]
        if part == 0:
            pl.semaphore_wait(barrier, len(partners))
        for k, peer in enumerate(others):
            sent.append(
                start_send(stage.at[part, k], got[part].at[me], send_sem.at[part, k], recv_sem.at[part, k],
                           at(peer))
            )
    for load in loads[1:]:
        load.wait()
    piece = block_rows // PARTS
    part_rows = blocks * piece
    for part in range(PARTS):
        for i in range(blocks):
            cot_parts[part, i * piece : (i + 1) * piece] = cot[
                i * block_rows + part * piece : i * block_rows + (part + 1) * piece
            ]
    w_hidden_t[...] = w_hidden[...].astype(F32).T.astype(BF16)
    w_output_t[...] = w_output[...].astype(F32).T.astype(BF16)
    for part in range(PARTS):
        dact[:, part * part_rows : (part + 1) * part_rows] = dot_rows(w_output[...], cot_parts[part])

    query_rows = PATCH_BLOCKS * piece
    pieces_sent = PARTS // SENDS
    for part in range(SENDS):
        for copy in sent[part * (peers - 1) : (part + 1) * (peers - 1)]:
            copy.wait_recv()
        for j in range(blocks):
            block = got[part][src[j]]
            for q in range(pieces_sent):
                start = j // PATCH_BLOCKS * patch + (part * pieces_sent + q) * query_rows + j % PATCH_BLOCKS * piece
                feats[start : start + piece] = block[q * piece : (q + 1) * piece]
        for first in range(0, rows, patch):
            these = slice(first + part * patch // SENDS, first + (part + 1) * patch // SENDS)
            qkv[these] = dot(feats[these], w_qkv[...]).astype(BF16)

    returned = []
    for part in range(PARTS):
        att[...] = jnp.zeros_like(att)
        for n in range(rows // patch):
            some_queries(qkv, att, n * patch, patch, n * patch + part * query_rows, query_rows, n * query_rows)
        packed[part] = att[...].astype(BF16).reshape(blocks, piece, D)
        for k, peer in enumerate(others):
            back_stage[part, k] = packed[part, block_for(src, peer)]
            returned.append(
                start_send(back_stage.at[part, k], back[part].at[me], back_send.at[part, k],
                           back_recv.at[part, k], at(peer))
            )
        back[part][me] = packed[part, block_for(src, me)]

    chunks = w_hidden_t.shape[0] // UNITS
    share = UNITS * peers // w_hidden_t.shape[0]
    units = UNITS // share
    pairs = share // 2
    quarter = units // xs
    pair, along_x = [], ([], [])

    def to_pair(chunk):
        for j in range(pairs):
            pair.append(
                start_send(terms.at[chunk * share + 2 * j + (1 - core)], pair_in.at[chunk * pairs + j],
                           pair_send.at[chunk * pairs + j], pair_recv.at[chunk * pairs + j], at(y * 2 + 1 - core))
            )

    def to_x(chunk, half):
        for j in range(pairs):
            if half == 0:
                pair[chunk * pairs + j].wait_recv()
            side = slice(half * units, (half + 1) * units)
            both = (
                terms[chunk * share + 2 * j + core, side].astype(F32)
                + pair_in[chunk * pairs + j, side].astype(F32)
            ).astype(BF16)
            for t in range(xs):
                x_out[half, chunk, t, j] = both[t * quarter : (t + 1) * quarter]
        for k in range(1, xs):
            along_x[half].append(
                start_send(x_out.at[half, chunk, (x + k) % xs], x_in.at[half, chunk, k - 1],
                           x_send.at[half, chunk, k - 1], x_recv.at[half, chunk, k - 1], on_x((x + k) % xs))
            )

    for part in range(PARTS):
        for copy in returned[part * (peers - 1) : (part + 1) * (peers - 1)]:
            copy.wait_recv()
        mixed = jnp.concatenate([back[part][dest[i]] for i in range(blocks)], axis=0)
        before = jnp.concatenate([points[i, part * piece : (part + 1) * piece] for i in range(blocks)], axis=0)
        hidden = (before.astype(F32) + dot(mixed, w_out[...])).astype(BF16)
        second[...] = (layer_norm(hidden.astype(F32)) * norm_mlp[...]).astype(BF16)
        these = slice(part * part_rows, (part + 1) * part_rows)
        for chunk in range(chunks):
            span = slice(chunk * UNITS, (chunk + 1) * UNITS)
            act, slope = gelu_and_slope(dot_rows(w_hidden_t[span], second[...]))
            act = act.astype(BF16)
            dpre = (dact[span, these] * slope).astype(BF16)
            out_part, hid_part = dot(act, cot_parts[part]), dot(dpre, second[...])
            if part:
                out_part, hid_part = out_acc[span] + out_part, hid_acc[span] + hid_part
            if part < PARTS - 1:
                out_acc[span], hid_acc[span] = out_part, hid_part
            else:
                for j in range(share):
                    mine = slice(j * units, (j + 1) * units)
                    terms[chunk * share + j, :units] = hid_part[mine].astype(BF16)
                    terms[chunk * share + j, units:] = out_part[mine].astype(BF16)
                to_pair(chunk)
                if chunk:
                    to_x(chunk - 1, 0)
            added = dot(w_output_t[:, span], act)
            result[...] = added if chunk == 0 else result[...] + added
        if part == PARTS - 1:
            to_x(chunks - 1, 0)
            for chunk in range(chunks):
                to_x(chunk, 1)
        ended = (hidden.astype(F32) + result[...].T).astype(BF16)
        for i in range(blocks):
            answer[i, part * piece : (part + 1) * piece] = ended[i * piece : (i + 1) * piece]
    store = pltpu.make_async_copy(answer, out_any, out_sem)
    store.start()

    along_y, along_z, last = ([], []), ([], []), ([], [])
    for half in range(2):
        for copy in along_x[half]:
            copy.wait_recv()
        for chunk in range(chunks):
            for j in range(pairs):
                mine = x_out[half, chunk, x, j].astype(F32)
                for k in range(xs - 1):
                    mine = mine + x_in[half, chunk, k, j].astype(F32)
                y_out[half, chunk * pairs + j] = mine.astype(BF16)
        for k in range(1, ys):
            along_y[half].append(
                start_send(y_out.at[half, (y + k) % ys], y_in.at[half, k - 1], y_send.at[half, k - 1],
                           y_recv.at[half, k - 1], at((y + k) % ys * 2 + core))
            )
    for half in range(2):
        mine = y_out[half, y].astype(F32)
        for k, copy in enumerate(along_y[half]):
            copy.wait_recv()
            mine = mine + y_in[half, k].astype(F32)
        z_all[half, z] = mine.astype(BF16)
        for k in range(1, zs):
            along_z[half].append(
                start_send(z_all.at[half, z], z_all.at[half, z], z_send.at[half, k - 1],
                           z_recv.at[half, k - 1], on_z((z + k) % zs))
            )
    for half in range(2):
        for copy in along_z[half]:
            copy.wait_recv()
        total = z_all[half, 0].astype(F32)
        for k in range(1, zs):
            total = total + z_all[half, k].astype(F32)
        x_all[half, x] = total * scale
        for k in range(1, xs):
            last[half].append(
                start_send(x_all.at[half, x], x_all.at[half, x], g_send.at[half, k - 1],
                           g_recv.at[half, k - 1], on_x((x + k) % xs))
            )
    for half, grad in enumerate((hidden_grad, output_grad)):
        for copy in last[half]:
            copy.wait_recv()
        grad[...] = x_all[half].reshape(units, D)
    both = [copy for stage in (along_x, along_y, along_z, last) for half in stage for copy in half]
    for copy in [*sent, *returned, *pair, *both]:
        copy.wait_send()
    store.wait()


def per_device(
    points, cotangent, dest_code, src_code, w_qkv, w_out, norm_attn, norm_mlp, w_hidden, w_output
):
    peers, groups = lax.axis_size("peer"), lax.axis_size("group")
    xs = 4 if groups % 4 == 0 else 1
    ys, zs = peers // 2, groups // xs
    blocks, rows = dest_code.shape[0], points.shape[0]
    block_rows, ff = rows // blocks, w_output.shape[0]
    scale = float(1.0 / np.sqrt(np.float32(rows * peers * groups)))
    units = ff // peers
    chunks, pairs = ff // UNITS, UNITS // units // 2
    quarter = units // xs
    vmem, smem = pl.BlockSpec(memory_space=pltpu.VMEM), pl.BlockSpec(memory_space=pltpu.SMEM)
    far = pl.BlockSpec(memory_space=pl.ANY)
    dma = pltpu.SemaphoreType.DMA
    some = max(xs - 1, 1)
    held = lambda shape, dtype=BF16: pltpu.VMEM(shape, dtype)
    result, hidden_grad, output_grad = pl.pallas_call(
        functools.partial(block_kernel, peers, xs, zs, scale),
        out_shape=(
            jax.ShapeDtypeStruct((blocks, block_rows, D), BF16),
            jax.ShapeDtypeStruct((units, D), F32),
            jax.ShapeDtypeStruct((units, D), F32),
        ),
        in_specs=[far, far, smem, smem, far, far, vmem, vmem, far, far],
        out_specs=(far, vmem, vmem),
        scratch_shapes=[
            held((blocks, block_rows, D)), held((rows, D)), held((D, 3 * D)), held((D, D)),
            held((D, ff)), held((ff, D)), held((ff, D)), held((D, ff)),
            held((PARTS, rows // PARTS, D)),
            held((SENDS, blocks, block_rows // SENDS, D)),
            held((SENDS, peers - 1, block_rows // SENDS, D)),
            (held((peers, block_rows // SENDS, D)),) * SENDS,
            held((rows, D)), held((rows, 3 * D)), held((rows // PARTS, D), F32),
            held((PARTS, blocks, block_rows // PARTS, D)),
            held((PARTS, peers - 1, block_rows // PARTS, D)),
            (held((peers, block_rows // PARTS, D)),) * PARTS,
            held((rows // PARTS, D)),
            held((ff, rows), F32), held((D, rows // PARTS), F32), held((blocks, block_rows, D)),
            held((ff, D), F32), held((ff, D), F32),
            held((peers, 2 * units, D)), held((ys, 2 * units, D)),
            held((2, chunks, xs, pairs, quarter, D)), held((2, chunks, some, pairs, quarter, D)),
            held((2, ys, quarter, D)), held((2, ys - 1, quarter, D)),
            held((2, zs, quarter, D)), held((2, xs, quarter, D), F32),
            dma((6,)), dma((SENDS, peers - 1)), dma((SENDS, peers - 1)),
            dma((PARTS, peers - 1)), dma((PARTS, peers - 1)),
            dma((ys,)), dma((ys,)), dma((2, chunks, some)), dma((2, chunks, some)),
            dma((2, ys - 1)), dma((2, ys - 1)), dma((2, max(zs - 1, 1))), dma((2, max(zs - 1, 1))),
            dma((2, some)), dma((2, some)), dma(()),
        ],
        compiler_params=pltpu.CompilerParams(
            collective_id=0, has_side_effects=True, vmem_limit_bytes=56 << 20
        ),
        cost_estimate=pl.CostEstimate(flops=1 << 33, bytes_accessed=4 << 20, transcendentals=1 << 23),
    )(points.reshape(blocks, block_rows, D), cotangent, dest_code, src_code, w_qkv, w_out,
      norm_attn.reshape(1, D), norm_mlp.reshape(1, D), w_hidden, w_output)
    return result.reshape(rows, D), hidden_grad.T, output_grad


def solution(mesh):
    return jax.shard_map(
        per_device,
        mesh=mesh,
        in_specs=(
            P(("group", "peer"), None),
            P(("group", "peer"), None),
            P(("group", "peer")),
            P(("group", "peer")),
            P(),
            P(),
            P(),
            P(),
            P(),
            P(),
        ),
        out_specs=(P(("group", "peer"), None), P(None, "peer"), P("peer", None)),
        check_vma=False,
    )
```

```python
import functools

import jax
import jax.numpy as jnp
import numpy as np
from jax import lax
from jax.experimental import pallas as pl
from jax.experimental.pallas import tpu as pltpu
from jax.sharding import PartitionSpec as P

D = 256
HEAD_DIM = 16
PATCH_BLOCKS = 4
LANES = 128
PARTS = 4
SENDS = 2
UNITS = 256
MESH = pl.DeviceIdType.MESH
F32, BF16 = jnp.float32, jnp.bfloat16


def layer_norm(v):
    centre = v - jnp.mean(v, axis=-1, keepdims=True)
    spread = jnp.mean(centre * centre, axis=-1, keepdims=True)
    return centre * lax.rsqrt(spread + 1e-05)


def dot(a, b):
    return jnp.dot(a, b, preferred_element_type=F32)


def dot_rows(a, b):
    return lax.dot_general(a, b, (((1,), (1,)), ((), ())), preferred_element_type=F32)


def gelu_and_slope(x):
    root = 0.7978845608028654
    square = x * x
    bend = jnp.tanh(x * (root + (root * 0.044715) * square))
    half = 0.5 + 0.5 * bend
    slope = half + (0.5 * x) * (1.0 - bend * bend) * (root + (3 * root * 0.044715) * square)
    return x * half, slope


def start_send(src, dst, send_sem, recv_sem, device):
    copy = pltpu.make_async_remote_copy(
        src_ref=src, dst_ref=dst, send_sem=send_sem, recv_sem=recv_sem,
        device_id=device, device_id_type=MESH,
    )
    copy.start()
    return copy


def far_first(count):
    return sorted(range(1, count), key=lambda k: -min(k, count - k))


def block_for(codes, peer):
    which = jnp.int32(0)
    for i in range(codes.shape[0]):
        which = jnp.where(codes[i] == peer, i, which)
    return which


def some_queries(qkv, att, first_key, keys_count, first_query, queries, first_out):
    head_of_lane = lax.broadcasted_iota(jnp.int32, (1, LANES), 1) // HEAD_DIM
    ones = jnp.ones((keys_count, LANES), BF16)
    factor = 1.4426950408889634 / HEAD_DIM**0.5
    zero = jnp.bfloat16(0)
    patch = slice(first_key, first_key + keys_count)
    these = slice(first_query, first_query + queries)
    outs = slice(first_out, first_out + queries)
    for lanes in range(0, D, LANES):

        def one_head(head, carry):
            mine = head_of_lane == head
            keys = qkv[patch, D + lanes : D + lanes + LANES]
            values = qkv[patch, 2 * D + lanes : 2 * D + lanes + LANES]
            values = jnp.concatenate([jnp.where(mine, values, zero), ones], axis=1)
            query = jnp.where(mine, qkv[these, lanes : lanes + LANES], zero)
            scores = dot_rows(query, keys)
            top = jnp.max(scores, axis=1, keepdims=True)
            weights = jnp.exp2((scores - top) * factor).astype(BF16)
            mixed = dot(weights, values)
            att[outs, lanes : lanes + LANES] += mixed[:, :LANES] / mixed[:, LANES:]
            return carry

        lax.fori_loop(0, LANES // HEAD_DIM, one_head, 0, unroll=LANES // HEAD_DIM)


def block_kernel(peers, xs, zs, scale, points_any, cot_any, dest, src, w_qkv_any, w_out_any, norm_attn,
                 norm_mlp, w_hidden_any, w_output_any, out_any, hidden_grad, output_grad,
                 points, cot, w_qkv, w_out, w_hidden, w_output, w_hidden_t, w_output_t,
                 cot_parts, normed, stage, got, feats, qkv, att, packed, back_stage, back, second,
                 dact, result, answer, out_acc, hid_acc, terms, pair_in, x_out, x_in, y_out, y_in, z_all, x_all,
                 load_sem, send_sem, recv_sem, back_send, back_recv, pair_send, pair_recv,
                 x_send, x_recv, y_send, y_recv, z_send, z_recv, g_send, g_recv, out_sem):
    loads = [
        pltpu.make_async_copy(a, b, load_sem.at[i])
        for i, (a, b) in enumerate(
            [(points_any, points), (w_qkv_any, w_qkv), (w_out_any, w_out), (cot_any, cot),
             (w_hidden_any, w_hidden), (w_output_any, w_output)]
        )
    ]
    for load in loads:
        load.start()
    group, me = lax.axis_index("group"), lax.axis_index("peer")
    ys = peers // 2
    y, core = me // 2, me % 2
    x, z = group // zs, group % zs
    blocks, block_rows = points.shape[0], points.shape[1]
    rows = blocks * block_rows
    patch = PATCH_BLOCKS * block_rows
    others = [(me + k) % peers for k in far_first(peers)]

    def at(peer):
        return {"group": group, "peer": peer}

    def on_x(other):
        return {"group": other * zs + z, "peer": me}

    def on_z(other):
        return {"group": x * zs + other, "peer": me}

    partners = [at(peer) for peer in others]
    partners += [on_x((x + k) % xs) for k in range(1, xs)]
    partners += [on_z((z + k) % zs) for k in range(1, zs)]
    barrier = pltpu.get_barrier_semaphore()
    for device in partners:
        pl.semaphore_signal(barrier, inc=1, device_id=device, device_id_type=MESH)

    loads[0].wait()
    step = block_rows // SENDS
    sent = []
    for part in range(SENDS):
        span = slice(part * step, (part + 1) * step)
        for i in range(blocks):
            normed[part, i] = (layer_norm(points[i, span].astype(F32)) * norm_attn[...]).astype(BF16)
        for k, peer in enumerate(others):
            stage[part, k] = normed[part, block_for(dest, peer)]
        got[part][me] = normed[part, block_for(dest, me)]
        if part == 0:
            pl.semaphore_wait(barrier, len(partners))
        for k, peer in enumerate(others):
            sent.append(
                start_send(stage.at[part, k], got[part].at[me], send_sem.at[part, k], recv_sem.at[part, k],
                           at(peer))
            )
    for load in loads[1:]:
        load.wait()
    piece = block_rows // PARTS
    part_rows = blocks * piece
    for part in range(PARTS):
        for i in range(blocks):
            cot_parts[part, i * piece : (i + 1) * piece] = cot[
                i * block_rows + part * piece : i * block_rows + (part + 1) * piece
            ]
    w_hidden_t[...] = w_hidden[...].astype(F32).T.astype(BF16)
    w_output_t[...] = w_output[...].astype(F32).T.astype(BF16)
    for part in range(PARTS):
        dact[:, part * part_rows : (part + 1) * part_rows] = dot_rows(w_output[...], cot_parts[part])

    query_rows = PATCH_BLOCKS * piece
    pieces_sent = PARTS // SENDS
    for part in range(SENDS):
        for copy in sent[part * (peers - 1) : (part + 1) * (peers - 1)]:
            copy.wait_recv()
        for j in range(blocks):
            block = got[part][src[j]]
            for q in range(pieces_sent):
                start = j // PATCH_BLOCKS * patch + (part * pieces_sent + q) * query_rows + j % PATCH_BLOCKS * piece
                feats[start : start + piece] = block[q * piece : (q + 1) * piece]
        for first in range(0, rows, patch):
            these = slice(first + part * patch // SENDS, first + (part + 1) * patch // SENDS)
            qkv[these] = dot(feats[these], w_qkv[...]).astype(BF16)

    returned = []
    for part in range(PARTS):
        att[...] = jnp.zeros_like(att)
        for n in range(rows // patch):
            some_queries(qkv, att, n * patch, patch, n * patch + part * query_rows, query_rows, n * query_rows)
        packed[part] = att[...].astype(BF16).reshape(blocks, piece, D)
        for k, peer in enumerate(others):
            back_stage[part, k] = packed[part, block_for(src, peer)]
            returned.append(
                start_send(back_stage.at[part, k], back[part].at[me], back_send.at[part, k],
                           back_recv.at[part, k], at(peer))
            )
        back[part][me] = packed[part, block_for(src, me)]

    chunks = w_hidden_t.shape[0] // UNITS
    share = UNITS * peers // w_hidden_t.shape[0]
    units = UNITS // share
    pairs = share // 2
    quarter = units // xs
    pair, along_x = [], ([], [])

    def to_pair(chunk):
        for j in range(pairs):
            pair.append(
                start_send(terms.at[chunk * share + 2 * j + (1 - core)], pair_in.at[chunk * pairs + j],
                           pair_send.at[chunk * pairs + j], pair_recv.at[chunk * pairs + j], at(y * 2 + 1 - core))
            )

    def to_x(chunk, half):
        for j in range(pairs):
            if half == 0:
                pair[chunk * pairs + j].wait_recv()
            side = slice(half * units, (half + 1) * units)
            both = (
                terms[chunk * share + 2 * j + core, side].astype(F32)
                + pair_in[chunk * pairs + j, side].astype(F32)
            ).astype(BF16)
            for t in range(xs):
                x_out[half, chunk, t, j] = both[t * quarter : (t + 1) * quarter]
        for k in far_first(xs):
            along_x[half].append(
                start_send(x_out.at[half, chunk, (x + k) % xs], x_in.at[half, chunk, k - 1],
                           x_send.at[half, chunk, k - 1], x_recv.at[half, chunk, k - 1], on_x((x + k) % xs))
            )

    for part in range(PARTS):
        for copy in returned[part * (peers - 1) : (part + 1) * (peers - 1)]:
            copy.wait_recv()
        mixed = jnp.concatenate([back[part][dest[i]] for i in range(blocks)], axis=0)
        before = jnp.concatenate([points[i, part * piece : (part + 1) * piece] for i in range(blocks)], axis=0)
        hidden = (before.astype(F32) + dot(mixed, w_out[...])).astype(BF16)
        second[...] = (layer_norm(hidden.astype(F32)) * norm_mlp[...]).astype(BF16)
        these = slice(part * part_rows, (part + 1) * part_rows)
        for chunk in range(chunks):
            span = slice(chunk * UNITS, (chunk + 1) * UNITS)
            act, slope = gelu_and_slope(dot_rows(w_hidden_t[span], second[...]))
            act = act.astype(BF16)
            dpre = (dact[span, these] * slope).astype(BF16)
            out_part, hid_part = dot(act, cot_parts[part]), dot(dpre, second[...])
            if part:
                out_part, hid_part = out_acc[span] + out_part, hid_acc[span] + hid_part
            if part < PARTS - 1:
                out_acc[span], hid_acc[span] = out_part, hid_part
            else:
                for j in range(share):
                    mine = slice(j * units, (j + 1) * units)
                    terms[chunk * share + j, :units] = hid_part[mine].astype(BF16)
                    terms[chunk * share + j, units:] = out_part[mine].astype(BF16)
                to_pair(chunk)
                if chunk:
                    to_x(chunk - 1, 0)
            added = dot(w_output_t[:, span], act)
            result[...] = added if chunk == 0 else result[...] + added
        if part == PARTS - 1:
            to_x(chunks - 1, 0)
            for chunk in range(chunks):
                to_x(chunk, 1)
        ended = (hidden.astype(F32) + result[...].T).astype(BF16)
        for i in range(blocks):
            answer[i, part * piece : (part + 1) * piece] = ended[i * piece : (i + 1) * piece]
    store = pltpu.make_async_copy(answer, out_any, out_sem)
    store.start()

    along_y, along_z, last = ([], []), ([], []), ([], [])
    for half in range(2):
        for copy in along_x[half]:
            copy.wait_recv()
        for chunk in range(chunks):
            for j in range(pairs):
                mine = x_out[half, chunk, x, j].astype(F32)
                for k in range(xs - 1):
                    mine = mine + x_in[half, chunk, k, j].astype(F32)
                y_out[half, chunk * pairs + j] = mine.astype(BF16)
        for k in far_first(ys):
            along_y[half].append(
                start_send(y_out.at[half, (y + k) % ys], y_in.at[half, k - 1], y_send.at[half, k - 1],
                           y_recv.at[half, k - 1], at((y + k) % ys * 2 + core))
            )
    for half in range(2):
        mine = y_out[half, y].astype(F32)
        for copy in along_y[half]:
            copy.wait_recv()
        for k in range(ys - 1):
            mine = mine + y_in[half, k].astype(F32)
        z_all[half, z] = mine.astype(BF16)
        for k in far_first(zs):
            along_z[half].append(
                start_send(z_all.at[half, z], z_all.at[half, z], z_send.at[half, k - 1],
                           z_recv.at[half, k - 1], on_z((z + k) % zs))
            )
    for half in range(2):
        for copy in along_z[half]:
            copy.wait_recv()
        total = z_all[half, 0].astype(F32)
        for k in range(1, zs):
            total = total + z_all[half, k].astype(F32)
        x_all[half, x] = total * scale
        for k in far_first(xs):
            last[half].append(
                start_send(x_all.at[half, x], x_all.at[half, x], g_send.at[half, k - 1],
                           g_recv.at[half, k - 1], on_x((x + k) % xs))
            )
    for half, grad in enumerate((hidden_grad, output_grad)):
        for copy in last[half]:
            copy.wait_recv()
        grad[...] = x_all[half].reshape(units, D)
    both = [copy for stage in (along_x, along_y, along_z, last) for half in stage for copy in half]
    for copy in [*sent, *returned, *pair, *both]:
        copy.wait_send()
    store.wait()


def per_device(
    points, cotangent, dest_code, src_code, w_qkv, w_out, norm_attn, norm_mlp, w_hidden, w_output
):
    peers, groups = lax.axis_size("peer"), lax.axis_size("group")
    xs = 4 if groups % 4 == 0 else 1
    ys, zs = peers // 2, groups // xs
    blocks, rows = dest_code.shape[0], points.shape[0]
    block_rows, ff = rows // blocks, w_output.shape[0]
    scale = float(1.0 / np.sqrt(np.float32(rows * peers * groups)))
    units = ff // peers
    chunks, pairs = ff // UNITS, UNITS // units // 2
    quarter = units // xs
    vmem, smem = pl.BlockSpec(memory_space=pltpu.VMEM), pl.BlockSpec(memory_space=pltpu.SMEM)
    far = pl.BlockSpec(memory_space=pl.ANY)
    dma = pltpu.SemaphoreType.DMA
    some = max(xs - 1, 1)
    held = lambda shape, dtype=BF16: pltpu.VMEM(shape, dtype)
    result, hidden_grad, output_grad = pl.pallas_call(
        functools.partial(block_kernel, peers, xs, zs, scale),
        out_shape=(
            jax.ShapeDtypeStruct((blocks, block_rows, D), BF16),
            jax.ShapeDtypeStruct((units, D), F32),
            jax.ShapeDtypeStruct((units, D), F32),
        ),
        in_specs=[far, far, smem, smem, far, far, vmem, vmem, far, far],
        out_specs=(far, vmem, vmem),
        scratch_shapes=[
            held((blocks, block_rows, D)), held((rows, D)), held((D, 3 * D)), held((D, D)),
            held((D, ff)), held((ff, D)), held((ff, D)), held((D, ff)),
            held((PARTS, rows // PARTS, D)),
            held((SENDS, blocks, block_rows // SENDS, D)),
            held((SENDS, peers - 1, block_rows // SENDS, D)),
            (held((peers, block_rows // SENDS, D)),) * SENDS,
            held((rows, D)), held((rows, 3 * D)), held((rows // PARTS, D), F32),
            held((PARTS, blocks, block_rows // PARTS, D)),
            held((PARTS, peers - 1, block_rows // PARTS, D)),
            (held((peers, block_rows // PARTS, D)),) * PARTS,
            held((rows // PARTS, D)),
            held((ff, rows), F32), held((D, rows // PARTS), F32), held((blocks, block_rows, D)),
            held((ff, D), F32), held((ff, D), F32),
            held((peers, 2 * units, D)), held((ys, 2 * units, D)),
            held((2, chunks, xs, pairs, quarter, D)), held((2, chunks, some, pairs, quarter, D)),
            held((2, ys, quarter, D)), held((2, ys - 1, quarter, D)),
            held((2, zs, quarter, D)), held((2, xs, quarter, D), F32),
            dma((6,)), dma((SENDS, peers - 1)), dma((SENDS, peers - 1)),
            dma((PARTS, peers - 1)), dma((PARTS, peers - 1)),
            dma((ys,)), dma((ys,)), dma((2, chunks, some)), dma((2, chunks, some)),
            dma((2, ys - 1)), dma((2, ys - 1)), dma((2, max(zs - 1, 1))), dma((2, max(zs - 1, 1))),
            dma((2, some)), dma((2, some)), dma(()),
        ],
        compiler_params=pltpu.CompilerParams(
            collective_id=0, has_side_effects=True, vmem_limit_bytes=56 << 20
        ),
        cost_estimate=pl.CostEstimate(flops=1 << 33, bytes_accessed=4 << 20, transcendentals=1 << 23),
    )(points.reshape(blocks, block_rows, D), cotangent, dest_code, src_code, w_qkv, w_out,
      norm_attn.reshape(1, D), norm_mlp.reshape(1, D), w_hidden, w_output)
    return result.reshape(rows, D), hidden_grad.T, output_grad


def solution(mesh):
    return jax.shard_map(
        per_device,
        mesh=mesh,
        in_specs=(
            P(("group", "peer"), None),
            P(("group", "peer"), None),
            P(("group", "peer")),
            P(("group", "peer")),
            P(),
            P(),
            P(),
            P(),
            P(),
            P(),
        ),
        out_specs=(P(("group", "peer"), None), P(None, "peer"), P("peer", None)),
        check_vma=False,
    )
```
